32 devices in a mesh: dom: 8 (over z, y), group: 4 (over x, core).
Axes of the slice: x: 2, y: 2, z: 4, core: 2. Of those that a mesh axis runs over, the one named last changes fastest.
Arguments:
- features: bfloat16 [4096, 1024], P(('dom', 'group')), may hold values from -6 to 6
- out_grad: bfloat16 [4096, 1024], P(('dom', 'group')), may hold values from -0.1796875 to 0.1796875
- gcn_weight: bfloat16 [1024, 1024], replicated, may hold values from -0.1875 to 0.1875
- tile_index: int32 [32, 4], P(('dom', 'group')), may hold values from 0 to 2
- tile_edges: int32 [32, 4, 128, 128], P(('dom', 'group')), may hold values 0 or 1
- halo_rows: int32 [8, 4, 8, 32], P('dom', 'group'), may hold values from 0 to 127
- routes: int32 [4096, 2], P(('dom', 'group')), may hold values from 0 to 15, all different within a row; in each aligned block of 128 rows (0 to 127, 128 to 255, ...) at most 20 rows name the same one
- route_weight: float32 [4096, 2], P(('dom', 'group')), may hold values from 0.25 to 1
- up_weight: bfloat16 [16, 1024, 4096], P('dom', None, 'group'), may hold values from -0.1875 to 0.1875
- down_weight: bfloat16 [16, 4096, 1024], P('dom', 'group'), may hold values from -0.09375 to 0.09375
Outputs:
- node_out: bfloat16 [4096, 1024], P(('dom', 'group'))
- up_grad: bfloat16 [16, 1024, 4096], P('dom', None, 'group')
- down_grad: bfloat16 [16, 4096, 1024], P('dom', 'group')
The draws below stay inside these ranges and needn't reach their ends.
Inputs may be any that keep to these rules, and one draw needn't show every extreme that they name: `routes`: in the rows of one partition no expert is named more than 20 times, and in every draw some partition names some expert exactly 20 times.
All inputs are finite; a program needn't handle non-finite values. No bound on the sum of `tile_edges` on one device may be relied on, other than what follows from the above.
Results may differ from the reference program's by a relative error of at most 0.0071.
Values may be sent and summed in bfloat16 or wider, within the bound.
A program may use at most 128 MiB of HBM per device.

```python
import math
import jax
import jax.numpy as jnp
import numpy as np
from jax import lax

D = 1024
FF = 4096
TOP = 2
TILE = 128
SLOTS = 4
NODES_DEV = 128
FF_DEV = 1024
EXPERTS = 16
NODES = 4096
LTILES = 1
STILES = 3
HROWS = 32
CAP = 20
N_DOM = 8
N_GROUP = 4


def set_ends(drawn, stream_key, smallest, high):
    spot = [jax.random.randint(jax.random.fold_in(stream_key, axis), (), 0, length) for axis, length in enumerate(drawn.shape)]
    longest = drawn.shape.index(max(drawn.shape))
    neighbour = spot[:longest] + [(spot[longest] + 1) % drawn.shape[longest]] + spot[longest + 1:]
    return drawn.at[tuple(spot)].set(smallest).at[tuple(neighbour)].set(high)


def level_of(stream_key, extent, split, least, high):
    def one(position, blocks):
        draws = jax.random.uniform(jax.random.fold_in(jax.random.fold_in(stream_key, 6), position), (blocks,), jnp.float32, least / len(split), high / len(split))
        return jnp.repeat(jnp.exp(draws), extent[position] // blocks).reshape((-1,) + (1,) * (len(extent) - position - 1))

    level = one(*split[0])
    for cut in split[1:]:
        level = level * one(*cut)
    return level


def deal_out(stream_key, own, number, rows, count, top, bound, slope):
    ranking = jax.random.permutation(stream_key, count)
    crowded, common = portions_of(count, rows * top, bound, slope, True), portions_of(count, rows * top, bound, slope, False)
    places = jnp.arange(count)

    def named(lengths, offset_by):
        used = int((lengths > 0).sum())
        fixed = max(1, used // 4)
        passed = fixed + (places - fixed + offset_by * (used - fixed)) % max(1, count - fixed)
        return jnp.zeros((count,), jnp.int32).at[ranking[jnp.where(places < fixed, places, passed)]].set(jnp.asarray(lengths, jnp.int32))

    lengths = jnp.where(number % 4 == 0, named(crowded, number // 4), named(common, number - number // 4 - 1))
    mixed = jax.random.permutation(jax.random.fold_in(own, 3), count)
    donor, taker = mixed[0:count // 2 * 2:2], mixed[1:count // 2 * 2:2]
    room = jnp.minimum(lengths[donor] - 1, bound - lengths[taker]) // 2
    room = jnp.where((donor == ranking[0]) | (taker == ranking[0]) | (lengths[taker] == 0), 0, jnp.maximum(room, 0))
    passed = jax.random.randint(jax.random.fold_in(own, 4), (count // 2,), 0, 1 << 20) % (room + 1)
    lengths = lengths.at[donor].add(-passed).at[taker].add(passed)
    members = jnp.searchsorted(jnp.cumsum(lengths), jnp.arange(rows * top), side="right").astype(jnp.int32)
    listing = members.reshape(top, rows).T
    listing = listing[jax.random.permutation(jax.random.fold_in(own, 1), rows)]
    offset_by = jax.random.randint(jax.random.fold_in(own, 2), (rows, 1), 0, top)
    return jnp.take_along_axis(listing, (jnp.arange(top)[None, :] + offset_by) % top, axis=1)


def portions_of(count, total, bound, slope, full):
    portions = [(1 << 20) // math.isqrt(rank ** slope) + 1 for rank in range(1, count + 1)]
    largest = bound if full else min(bound, max(-(-total // count), total * portions[0] // sum(portions)))
    least = 1 if total - largest >= count - 1 else 0
    counts, rest = [largest] + [least] * (count - 1), total - largest - least * (count - 1)
    while rest > 0:
        candidates = [i for i in range(1, count) if counts[i] < largest] or [i for i in range(1, count) if counts[i] < bound]
        mass, budget = sum([portions[i] for i in candidates]), rest
        for i in candidates:
            more = min(bound - counts[i], max(1, budget * portions[i] // mass), rest)
            counts[i] = counts[i] + more
            rest = rest - more
    return np.array(counts)


def gaussian(stream_key, extent, scale, most, shards=(), kind=jnp.bfloat16):
    array = scale * jax.random.normal(stream_key, extent, jnp.float32)
    if shards:
        array = array * level_of(stream_key, extent, shards, -0.22, 0.18)
    return jnp.clip(array, -most, most).astype(kind)


def setup_inputs(seed: int = 0) -> dict:
    arg_keys = jax.random.split(jax.random.key(seed), 11)
    features = gaussian(arg_keys[0], (NODES, D), 1.0, 6.0, ((0, 32),))
    out_grad = gaussian(arg_keys[1], (NODES, D), 0.03, 0.1796875, ((0, 32),))
    gcn_weight = gaussian(arg_keys[2], (D, D), D ** -0.5, 0.1875)
    tile_index = set_ends(jax.random.randint(arg_keys[3], (NODES // TILE, SLOTS), 0, STILES), jax.random.fold_in(arg_keys[3], 1), 0, STILES - 1).astype(jnp.int32)
    tile_edges = set_ends((jax.random.randint(arg_keys[4], (NODES // TILE, SLOTS, TILE, TILE), 0, 16) < 1).astype(jnp.int32), jax.random.fold_in(arg_keys[4], 1), 0, 1)
    halo_rows = set_ends(jax.random.randint(arg_keys[5], (N_DOM, N_GROUP, N_DOM, HROWS), 0, NODES_DEV), jax.random.fold_in(arg_keys[5], 1), 0, NODES_DEV - 1).astype(jnp.int32)
    routes_keys = jax.random.split(jax.random.fold_in(arg_keys[6], 1), NODES // NODES_DEV)
    routes_turns = jax.random.permutation(jax.random.fold_in(arg_keys[6], 3), NODES // NODES_DEV)
    routes = jax.vmap(lambda own, number: deal_out(jax.random.fold_in(arg_keys[6], 2), own, number, NODES_DEV, EXPERTS, TOP, CAP, 2))(routes_keys, routes_turns).reshape((NODES, TOP))
    route_weight = jnp.clip(0.25 + 0.75 * jax.random.uniform(arg_keys[7], (NODES, TOP), jnp.float32) ** level_of(arg_keys[7], (NODES, TOP), ((0, 32),), -0.2, 0.2), 0.25, 1.0)
    up_weight = gaussian(arg_keys[8], (EXPERTS, D, FF), D ** -0.5, 0.1875, ((0, 8), (2, 4)))
    down_weight = gaussian(arg_keys[9], (EXPERTS, FF, D), FF ** -0.5, 0.09375, ((0, 8), (1, 4)))
    return dict(features=features, out_grad=out_grad, gcn_weight=gcn_weight, tile_index=tile_index, tile_edges=tile_edges, halo_rows=halo_rows, routes=routes, route_weight=route_weight, up_weight=up_weight, down_weight=down_weight)


def silu_slope(values):
    logistic = jax.nn.sigmoid(values)
    return logistic * (1.0 + values * (1.0 - logistic))

def slot_table(route_rows):
    flat_ids = route_rows.reshape(-1)
    onehot = (flat_ids[:, None] == jnp.arange(EXPERTS, dtype=jnp.int32)[None, :]).astype(jnp.int32)
    before = jnp.cumsum(onehot, axis=0) - onehot
    within = lax.optimization_barrier(jnp.sum(before * onehot, axis=1))
    target = flat_ids * CAP + within
    filler = jnp.zeros((EXPERTS * CAP,), jnp.int32).at[target].set(jnp.arange(flat_ids.shape[0], dtype=jnp.int32) + 1)
    return (target, filler)

def pick_rows(matrix, positions):
    return matrix[positions]

def aggregate(packed):
    source_tiles, index_row, edge_row, own_rows = packed
    chosen = source_tiles[index_row]
    summed = own_rows.reshape(LTILES, TILE, D).astype(jnp.float32) + jnp.einsum('tsij,tsjd->tid', edge_row.astype(jnp.float32), chosen.astype(jnp.float32))
    degree = 1.0 + lax.optimization_barrier(jnp.sum(edge_row, axis=(1, 3))).astype(jnp.float32)
    return (summed / jnp.sqrt(degree)[:, :, None]).reshape(NODES_DEV, D).astype(jnp.bfloat16)

def expert(packed):
    token_rows, cot_rows, up_matrix, down_matrix = packed
    count_rows = token_rows.shape[0]
    up_proj = jnp.dot(token_rows, up_matrix, preferred_element_type=jnp.float32)
    active = jax.nn.silu(up_proj).astype(jnp.bfloat16)
    blocks = jnp.einsum('rgf,gfd->rgd', active.reshape(count_rows, N_GROUP, FF_DEV).astype(jnp.float32), down_matrix.reshape(N_GROUP, FF_DEV, D).astype(jnp.float32))
    rounded = lax.optimization_barrier(blocks.astype(jnp.bfloat16)).astype(jnp.float32)
    expert_out = lax.optimization_barrier(jnp.sum(rounded, axis=1)).astype(jnp.bfloat16)
    grad_act = jnp.dot(cot_rows, down_matrix.T, preferred_element_type=jnp.float32)
    grad_pre = (grad_act * silu_slope(up_proj)).astype(jnp.bfloat16)
    down_part = jnp.dot(active.T, cot_rows, preferred_element_type=jnp.float32).astype(jnp.bfloat16)
    up_part = jnp.dot(token_rows.T, grad_pre, preferred_element_type=jnp.float32).astype(jnp.bfloat16)
    return (expert_out, up_part, down_part)

def reference(features, out_grad, gcn_weight, tile_index, tile_edges, halo_rows, routes, route_weight, up_weight, down_weight):
    devices = N_DOM * N_GROUP
    node_grid = features.reshape(N_DOM, N_GROUP, NODES_DEV, D)
    dom_ids = jnp.arange(N_DOM, dtype=jnp.int32)[:, None, None, None]
    group_ids = jnp.arange(N_GROUP, dtype=jnp.int32)[None, :, None, None]
    picked = node_grid[dom_ids, group_ids, halo_rows]
    border = jnp.transpose(picked, (2, 1, 0, 3, 4)).reshape(devices, N_DOM * HROWS, D)
    own_nodes = features.reshape(devices, NODES_DEV, D)
    sources = jnp.concatenate([own_nodes, border], axis=1).reshape(devices, STILES, TILE, D)
    aggregated = lax.map(aggregate, (sources, tile_index.reshape(devices, LTILES, SLOTS), tile_edges.reshape(devices, LTILES, SLOTS, TILE, TILE), own_nodes)).reshape(NODES, D)
    preact = jnp.dot(aggregated, gcn_weight, preferred_element_type=jnp.float32)
    hidden = (features.astype(jnp.float32) + jax.nn.silu(preact)).astype(jnp.bfloat16)
    targets, fillers = jax.vmap(slot_table)(routes.reshape(devices, NODES_DEV * TOP))
    cotangent = (route_weight[:, :, None] * out_grad[:, None, :].astype(jnp.float32)).astype(jnp.bfloat16).reshape(devices, NODES_DEV * TOP, D)
    hidden_dev = hidden.reshape(devices, NODES_DEV, D)
    present = (fillers > 0)[:, :, None]
    source_pair = jnp.maximum(fillers - 1, 0)
    nothing = jnp.zeros((), jnp.bfloat16)
    slot_hidden = jnp.where(present, jax.vmap(pick_rows)(hidden_dev, source_pair // TOP), nothing)
    slot_cot = jnp.where(present, jax.vmap(pick_rows)(cotangent, source_pair), nothing)
    expert_hidden = jnp.transpose(slot_hidden.reshape(devices, EXPERTS, CAP, D), (1, 0, 2, 3)).reshape(EXPERTS, devices * CAP, D)
    expert_cot = jnp.transpose(slot_cot.reshape(devices, EXPERTS, CAP, D), (1, 0, 2, 3)).reshape(EXPERTS, devices * CAP, D)
    expert_outs, up_grad, down_grad = lax.map(expert, (expert_hidden, expert_cot, up_weight, down_weight))
    returned = jnp.transpose(expert_outs.reshape(EXPERTS, devices, CAP, D), (1, 0, 2, 3)).reshape(devices, EXPERTS * CAP, D)
    gathered = jax.vmap(pick_rows)(returned, targets).reshape(NODES, TOP, D)
    node_out = (hidden.astype(jnp.float32) + lax.optimization_barrier(jnp.sum(route_weight[:, :, None] * gathered.astype(jnp.float32), axis=1))).astype(jnp.bfloat16)
    return (node_out, up_grad, down_grad)
```

```python
import functools

import jax
import jax.numpy as jnp
from jax import lax
from jax.experimental import pallas as pl
from jax.experimental.pallas import tpu as pltpu
from jax.sharding import PartitionSpec as P


def silu_slope(values):
    logistic = jax.nn.sigmoid(values)
    return logistic * (1.0 + values * (1.0 - logistic))


def capacity_of(node_count, top_count, expert_count):
    return max(2, 5 * node_count * top_count // (4 * expert_count))


def slot_table(route_rows, expert_count, capacity):
    flat_ids = route_rows.reshape(-1)
    order = jnp.arange(flat_ids.shape[0], dtype=jnp.int32)
    alike = (flat_ids[:, None] == flat_ids[None, :]) & (order[None, :] < order[:, None])
    within = jnp.sum(alike.astype(jnp.int32), axis=1)
    target = flat_ids * capacity + within
    filler = (
        jnp.zeros((expert_count * capacity,), jnp.int32)
        .at[target]
        .set(jnp.arange(flat_ids.shape[0], dtype=jnp.int32) + 1)
    )
    return (target, filler)


def local(
    features,
    out_grad,
    gcn_weight,
    tile_index,
    tile_edges,
    halo_rows,
    routes,
    route_weight,
    up_weight,
    down_weight,
):
    dom_count = lax.axis_size("dom")
    group_count = lax.axis_size("group")
    node_count, width = features.shape
    tile_rows = tile_edges.shape[-1]
    local_tiles = tile_index.shape[0]
    border_rows = halo_rows.shape[-1]
    expert_local = up_weight.shape[0]
    expert_count = expert_local * dom_count
    top_count = routes.shape[1]
    capacity = capacity_of(node_count, top_count, expert_count)
    send_lists = halo_rows.reshape(-1)
    outgoing = features[send_lists].reshape(dom_count, border_rows, width)
    incoming = lax.all_to_all(outgoing, "dom", split_axis=0, concat_axis=0, tiled=True)
    sources = jnp.concatenate(
        [features, incoming.reshape(dom_count * border_rows, width)], axis=0
    ).reshape(-1, tile_rows, width)
    source_tiles = sources.shape[0]
    listed = (tile_index[:, :, None] == jnp.arange(source_tiles, dtype=jnp.int32)).astype(jnp.int32)
    adjacency = jnp.sum(
        tile_edges[:, :, :, None, :] * listed[:, :, None, :, None], axis=1
    ).reshape(local_tiles, tile_rows, source_tiles * tile_rows)
    summed = features.reshape(local_tiles, tile_rows, width).astype(jnp.float32) + jnp.einsum(
        "tij,jd->tid",
        adjacency.astype(jnp.bfloat16),
        sources.reshape(source_tiles * tile_rows, width),
        preferred_element_type=jnp.float32,
    )
    degree = 1.0 + jnp.sum(tile_edges, axis=(1, 3)).astype(jnp.float32)
    aggregated = (
        (summed / jnp.sqrt(degree)[:, :, None]).reshape(node_count, width).astype(jnp.bfloat16)
    )
    preact = jnp.dot(aggregated, gcn_weight, preferred_element_type=jnp.float32)
    hidden = (features.astype(jnp.float32) + jax.nn.silu(preact)).astype(jnp.bfloat16)
    targets, fillers = slot_table(routes, expert_count, capacity)
    cotangent = (
        (route_weight[:, :, None] * out_grad[:, None, :].astype(jnp.float32))
        .astype(jnp.bfloat16)
        .reshape(-1, width)
    )
    present = (fillers > 0)[:, None]
    source_pair = jnp.maximum(fillers - 1, 0)
    nothing = jnp.zeros((), jnp.bfloat16)
    slot_shape = (dom_count, expert_local * capacity, width)
    send_hidden = jnp.where(present, hidden[source_pair // top_count], nothing).reshape(slot_shape)
    send_cot = jnp.where(present, cotangent[source_pair], nothing).reshape(slot_shape)
    mine_cot = lax.all_to_all(send_cot, "dom", split_axis=0, concat_axis=0, tiled=True)
    token_cot = lax.all_gather(mine_cot[None], "group", axis=0, tiled=True)
    mine_hidden = lax.all_to_all(send_hidden, "dom", split_axis=0, concat_axis=0, tiled=True)
    token_hidden = lax.all_gather(mine_hidden[None], "group", axis=0, tiled=True)
    sender_count = group_count * dom_count
    token_hidden = token_hidden.reshape(sender_count, expert_local, capacity, width)
    token_cot = token_cot.reshape(sender_count, expert_local, capacity, width)
    up_proj = jnp.einsum(
        "secd,edf->secf", token_hidden, up_weight, preferred_element_type=jnp.float32
    )
    active = jax.nn.silu(up_proj).astype(jnp.bfloat16)
    merged = lax.psum_scatter(
        jnp.einsum(
            "secf,efd->secd", active, down_weight, preferred_element_type=jnp.float32
        ).astype(jnp.bfloat16),
        "group",
        scatter_dimension=0,
        tiled=True,
    )
    expert_out = merged.reshape(dom_count, expert_local * capacity, width)
    returned = lax.all_to_all(expert_out, "dom", split_axis=0, concat_axis=0, tiled=True).reshape(
        expert_count * capacity, width
    )
    gathered = returned[targets].reshape(node_count, top_count, width)
    node_out = (
        hidden.astype(jnp.float32)
        + jnp.sum(route_weight[:, :, None] * gathered.astype(jnp.float32), axis=1)
    ).astype(jnp.bfloat16)
    grad_act = jnp.einsum(
        "secd,efd->secf", token_cot, down_weight, preferred_element_type=jnp.float32
    )
    grad_pre = (grad_act * silu_slope(up_proj)).astype(jnp.bfloat16)
    down_grad = jnp.einsum(
        "secf,secd->efd", active, token_cot, preferred_element_type=jnp.float32
    ).astype(jnp.bfloat16)
    up_grad = jnp.einsum(
        "secd,secf->edf", token_hidden, grad_pre, preferred_element_type=jnp.float32
    ).astype(jnp.bfloat16)
    return (node_out, up_grad, down_grad)


def dot(left, right, over=((1,), (0,))):
    return lax.dot_general(left, right, (over, ((), ())), preferred_element_type=jnp.float32)


def fused_kernel(
    doms,
    capacity,
    features,
    out_grad,
    gcn_weight,
    tile_index,
    edges,
    halo_rows,
    routes,
    route_weight,
    up_weight,
    down_weight,
    node_out,
    up_grad,
    down_grad,
    gcn,
    up,
    down,
    halo_send,
    sources,
    send,
    token,
    rows_hidden,
    rows_cot,
    active,
    grad_pre,
    partial,
    from_core,
    from_x,
    total,
    returned,
    hidden,
    weight_sem,
    halo_ss,
    halo_rs,
    slot_ss,
    slot_rs,
    fx_ss,
    fx_rs,
    fc_ss,
    fc_rs,
    fd_ss,
    fd_rs,
    core_ss,
    core_rs,
    x_ss,
    x_rs,
    ret_ss,
    ret_rs,
):
    f32, bf16 = jnp.float32, jnp.bfloat16
    dom, group = lax.axis_index("dom"), lax.axis_index("group")
    chip, core = group // 2, group % 2
    other_core = chip * 2 + (1 - core)
    other_chip = (1 - chip) * 2 + core
    nodes, width = features.shape
    borders = halo_rows.shape[1]
    block = 2 * capacity
    window = 24
    second = block - window
    slots = doms * block
    padded = -(-slots // 128) * 128
    experts = 2 * doms
    hidden_units = up.shape[2]
    half = doms // 2
    side = half * window
    batch = 2 * side
    step = 256

    def partner(d):
        place = 0
        for bit in (1, 2, 4):
            mine, theirs = lax.rem(lax.div(dom, bit), 2), lax.rem(lax.div(d, bit), 2)
            place = place + bit * (mine + theirs - 2 * mine * theirs)
        return place

    def own_border(place):
        return pl.ds(pl.multiple_of(nodes + place * borders, borders), borders)

    def remote(src, dst, ss, rs, **where):
        return pltpu.make_async_remote_copy(
            src_ref=src,
            dst_ref=dst,
            send_sem=ss,
            recv_sem=rs,
            device_id=where,
            device_id_type=pl.DeviceIdType.MESH,
        )

    def each(low, high, body):
        def one(place, carry):
            body(place)
            return carry

        lax.fori_loop(low, high, one, 0)

    def halo_copy(d):
        there = partner(d)
        return remote(
            halo_send.at[pl.ds(pl.multiple_of(there * borders, borders), borders)],
            sources.at[own_border(dom)],
            halo_ss.at[d],
            halo_rs.at[d],
            dom=there,
            group=group,
        )

    def halo_wait(d):
        there = partner(d)
        remote(
            halo_send.at[pl.ds(pl.multiple_of(there * borders, borders), borders)],
            sources.at[own_border(there)],
            halo_ss.at[d],
            halo_rs.at[d],
            dom=there,
            group=group,
        ).wait_recv()

    def slot(a, d):
        return remote(
            send.at[a, d],
            token.at[a, 0, d],
            slot_ss.at[a, d],
            slot_rs.at[a, d],
            dom=partner(d),
            group=group,
        )

    def forward(a, d, src, dst, to, ss, rs):
        return remote(
            token.at[a, src, d], token.at[a, dst, d], ss.at[a, d], rs.at[a, d], dom=dom, group=to
        )

    def to_chip(a, d):
        return forward(a, d, 0, 2, other_chip, fx_ss, fx_rs)

    def to_core(a, d):
        return forward(a, d, 0, 1, other_core, fc_ss, fc_rs)

    def relayed(a, d):
        return forward(a, d, 2, 3, other_core, fd_ss, fd_rs)

    def spread(a, d):
        to_chip(a, d).start()
        to_core(a, d).start()

    def pass_on(a, d):
        slot(a, d).wait_recv()
        spread(a, d)

    def relay(a, d):
        to_chip(a, d).wait_recv()
        relayed(a, d).start()

    def core_copy(which, h):
        return remote(
            partial.at[1 + 2 * which, pl.ds(h * half, half)],
            from_core.at[which, pl.ds(h * half, half)],
            core_ss.at[which, h],
            core_rs.at[which, h],
            dom=dom,
            group=other_core,
        )

    def x_copy(d):
        return remote(
            total.at[1, d], from_x.at[d], x_ss.at[d], x_rs.at[d], dom=dom, group=other_chip
        )

    def ret_copy(d):
        return remote(
            total.at[0, d], returned.at[d], ret_ss.at[d], ret_rs.at[d], dom=partner(d), group=group
        )

    row_of = lax.broadcasted_iota(jnp.int32, (window, 1), 0)
    keep = [
        jnp.where(row_of < capacity, 1.0, 0.0).astype(bf16),
        jnp.where(row_of >= window - capacity, 1.0, 0.0).astype(bf16),
    ]
    early = lax.broadcasted_iota(jnp.int32, (window - second, 1), 0) < capacity - second

    def rows_of(h, c):
        if c is None:
            return pl.ds(2 * h * batch, 2 * batch)
        return pl.ds((2 * h + c) * batch, batch)

    def take(a, h, c):
        target = rows_cot if a == 0 else rows_hidden
        for j in range(2):
            start = (2 * h + c) * batch + j * side
            for e in range(2):
                parts = []
                for k in range(half):
                    values = token[a, 2 * c + j, h * half + k, e * second : e * second + window, :]
                    if a == 0:
                        values = values * keep[e]
                    parts.append(values)
                target[e, start : start + side, :] = jnp.concatenate(parts, axis=0)

    def project(h, c, ready=False):
        rows = rows_of(h, c)

        def units(f):
            columns = pl.ds(pl.multiple_of(f * step, step), step)
            projs = [dot(rows_hidden[e, rows, :], up[e, :, columns]) for e in range(2)]
            for e, proj in enumerate(projs):
                gate = 0.5 + 0.5 * jnp.tanh(0.5 * proj)
                value = proj * gate
                active[e, rows, columns] = value.astype(bf16)
                slope = gate + value * (1.0 - gate)
                if ready:
                    slope = slope * grad_pre[e, rows, columns].astype(f32)
                grad_pre[e, rows, columns] = slope.astype(bf16)

        each(0, hidden_units // step, units)

    def combine(h, c):
        rows = rows_of(h, c)
        chips = (0, 1) if c is None else (c,)

        def outs(f):
            columns = pl.ds(pl.multiple_of(f * step, step), step)
            first = dot(active[0, rows, :], down[0, :, columns])
            last = dot(active[1, rows, :], down[1, :, columns])
            for n in range(len(chips) * 2 * half):
                at = n * window
                cut = at + second
                values = jnp.concatenate(
                    [
                        first[at:cut],
                        jnp.where(early, first[cut : at + window], last[at : at + window - second]),
                        last[at + window - second : at + window],
                    ],
                    axis=0,
                )
                rel = 2 * chips[n // (2 * half)] + n // half % 2
                partial[rel, h * half + n % half, :, columns] = values.astype(bf16)

        each(0, width // step, outs)

    def slopes(h, c, first=False):
        rows = rows_of(h, c)

        def units(f):
            columns = pl.ds(pl.multiple_of(f * step, step), step)
            grads = [dot(rows_cot[e, rows, :], down[e, columns, :], ((1,), (1,))) for e in range(2)]
            for e, grad in enumerate(grads):
                if not first:
                    grad = grad * grad_pre[e, rows, columns].astype(f32)
                grad_pre[e, rows, columns] = grad.astype(bf16)

        each(0, hidden_units // step, units)

    def down_grads(e, f):
        rows = pl.ds(pl.multiple_of(f * step, step), step)
        down_grad[e, rows, :] = dot(active[e, :, rows], rows_cot[e], ((0,), (0,))).astype(bf16)

    def up_grads(e, f):
        rows = pl.ds(pl.multiple_of(f * step, step), step)
        up_grad[e, rows, :] = dot(rows_hidden[e, :, rows], grad_pre[e], ((0,), (0,))).astype(bf16)

    def send_sum(d):
        total[1, d] = (partial[2, d].astype(f32) + from_core[1, d].astype(f32)).astype(bf16)
        x_copy(d).start()

    def sum_up(d):
        x_copy(d).wait_recv()
        return (
            partial[0, d].astype(f32) + from_core[0, d].astype(f32) + from_x[d].astype(f32)
        ).astype(bf16)

    def send_back(d):
        total[0, d] = sum_up(d)
        ret_copy(d).start()

    loads = [
        pltpu.make_async_copy(gcn_weight, gcn, weight_sem.at[0]),
        pltpu.make_async_copy(up_weight, up, weight_sem.at[2]),
        pltpu.make_async_copy(down_weight, down, weight_sem.at[1]),
    ]
    for load in loads:
        load.start()
    barrier = pltpu.get_barrier_semaphore()
    each(
        1,
        doms,
        lambda d: pl.semaphore_signal(
            barrier,
            inc=1,
            device_id={"dom": partner(d), "group": group},
            device_id_type=pl.DeviceIdType.MESH,
        ),
    )
    for peer in (other_core, other_chip):
        pl.semaphore_signal(
            barrier,
            inc=1,
            device_id={"dom": dom, "group": peer},
            device_id_type=pl.DeviceIdType.MESH,
        )

    own = features[...]
    node_of = lax.broadcasted_iota(jnp.int32, (nodes, borders), 0)
    picks = jnp.concatenate(
        [jnp.where(node_of == halo_rows[b : b + 1, :], 1.0, 0.0).T for b in range(doms)], axis=0
    ).astype(bf16)
    halo_send[...] = dot(picks, own).astype(bf16)
    expert_of = lax.broadcasted_iota(jnp.int32, (experts, nodes), 0)
    named = [jnp.where(expert_of == routes[k : k + 1, :], 1.0, 0.0) for k in range(2)]
    across = lax.broadcasted_iota(jnp.int32, (nodes, nodes), 0)
    along = lax.broadcasted_iota(jnp.int32, (nodes, nodes), 1)
    earlier = jnp.where(across < along, 1.0, 0.0).astype(bf16)
    before = dot((named[0] + named[1]).astype(bf16), earlier)
    slot_row = lax.broadcasted_iota(jnp.int32, (padded, nodes), 0).astype(f32)
    slotted, gates = [], []
    for k in range(2):
        within = jnp.sum(named[k] * before, axis=0, keepdims=True)
        chosen = routes[k : k + 1, :]
        chunk = ((chosen >> 1) ^ dom) * 2 + (chosen & 1)
        target = chunk.astype(f32) * capacity + within
        slotted.append(jnp.where(slot_row == target, 1.0, 0.0))
        gates.append(
            jnp.sum(jnp.where(across == along, route_weight[k : k + 1, :], 0.0), axis=1, keepdims=True)
        )
    gather = (slotted[0] + slotted[1]).astype(bf16)[0:slots, :]
    slot_gate = jnp.sum(
        slotted[0] * route_weight[0:1, :] + slotted[1] * route_weight[1:2, :],
        axis=1,
        keepdims=True,
    )[0:slots, :]

    def fill(a, values):
        for d in range(doms):
            part = values[d * block : (d + 1) * block].astype(bf16)
            send[a, d] = part
            if d == 0:
                token[a, 0, 0] = part

    fill(0, dot(gather, out_grad[...]) * slot_gate)
    pl.semaphore_wait(barrier, doms + 1)
    each(1, half, lambda d: slot(0, d).start())
    each(half, doms, lambda d: halo_copy(d).start())
    each(1, half, lambda d: halo_copy(d).start())
    sources[own_border(dom), :] = halo_send[
        pl.ds(pl.multiple_of(dom * borders, borders), borders), :
    ]
    spread(0, 0)

    near_tile = 1 + lax.div(dom, half)
    far_tile = 3 - near_tile

    def adjacency(t):
        found = jnp.zeros((nodes, nodes), f32)
        for s in range(edges.shape[0]):
            found = found + edges[s].astype(f32) * jnp.where(tile_index[0, s] == t, 1.0, 0.0)
        return found

    def tile(t):
        return sources[pl.ds(pl.multiple_of(t * nodes, nodes), nodes), :]

    matrix = [adjacency(t) for t in (0, near_tile, far_tile)]
    degree = 1.0 + jnp.sum(matrix[0] + matrix[1] + matrix[2], axis=1, keepdims=True)
    root = jnp.sqrt(degree)
    summed = own.astype(f32) + dot(matrix[0].astype(bf16), own)
    loads[0].wait()
    each(1, half, halo_wait)
    summed = summed + dot(matrix[1].astype(bf16), tile(near_tile))
    each(1, half, lambda d: pass_on(0, d))
    each(half, doms, halo_wait)
    summed = summed + dot(matrix[2].astype(bf16), tile(far_tile))
    aggregated = (summed / root).astype(bf16)
    preact = dot(aggregated, gcn[...])
    hidden[...] = (own.astype(f32) + preact / (1.0 + jnp.exp(-preact))).astype(bf16)
    fill(1, dot(gather, hidden[...]))
    each(1, half, lambda d: slot(1, d).start())
    each(half, doms, lambda d: slot(1, d).start())
    spread(1, 0)

    loads[1].wait()
    loads[2].wait()
    each(0, half, lambda d: to_core(0, d).wait_recv())
    take(0, 0, 0)
    each(0, half, lambda d: relay(0, d))
    each(0, half, lambda d: relayed(0, d).wait_recv())
    take(0, 0, 1)
    slopes(0, None, True)
    each(1, half, lambda d: pass_on(1, d))
    each(0, half, lambda d: to_core(1, d).wait_recv())
    take(1, 0, 0)
    project(0, 0, True)
    each(half, half + 2, lambda d: pass_on(1, d))
    each(half, doms, lambda d: slot(0, d).start())
    each(half + 2, doms, lambda d: pass_on(1, d))
    each(0, half, lambda d: relay(1, d))
    each(0, half, lambda d: relayed(1, d).wait_recv())
    take(1, 0, 1)
    project(0, 1, True)
    each(half, doms, lambda d: to_core(1, d).wait_recv())
    take(1, 1, 0)
    project(1, 0)
    combine(0, None)
    core_copy(1, 0).start()
    core_copy(0, 0).start()
    each(half, doms, lambda d: relay(1, d))
    each(half, doms, lambda d: relayed(1, d).wait_recv())
    take(1, 1, 1)
    project(1, 1)
    core_copy(1, 0).wait_recv()
    each(0, half, send_sum)
    combine(1, None)
    core_copy(1, 1).start()
    core_copy(0, 1).start()
    core_copy(1, 1).wait_recv()
    each(half, doms, send_sum)
    each(half, half + 2, lambda d: pass_on(0, d))
    core_copy(0, 0).wait_recv()
    each(1, half, send_back)
    returned[0] = sum_up(0)
    core_copy(0, 1).wait_recv()
    send_back(half)
    each(half + 2, doms, lambda d: pass_on(0, d))
    each(half + 1, doms, send_back)
    each(half, doms, lambda d: to_core(0, d).wait_recv())
    take(0, 1, 0)
    each(half, doms, lambda d: relay(0, d))
    each(half, doms, lambda d: relayed(0, d).wait_recv())
    take(0, 1, 1)
    slopes(1, None)
    for e in range(2):
        each(0, hidden_units // step, lambda f: down_grads(e, f))
        each(0, width // step, lambda f: up_grads(e, f))

    each(1, doms, lambda d: ret_copy(d).wait_recv())
    back = jnp.concatenate([returned[d].astype(f32) for d in range(doms)], axis=0).astype(bf16)
    mixed = jnp.zeros((nodes, width), f32)
    for k in range(2):
        mixed = mixed + gates[k] * dot(slotted[k].T[:, 0:slots].astype(bf16), back)
    node_out[...] = (hidden[...].astype(f32) + mixed).astype(bf16)

    def finish(d):
        halo_copy(d).wait_send()
        slot(0, d).wait_send()
        slot(1, d).wait_send()
        ret_copy(d).wait_send()

    each(1, doms, finish)

    def finish_rest(d):
        for a in range(2):
            to_chip(a, d).wait_send()
            to_core(a, d).wait_send()
            relayed(a, d).wait_send()
        x_copy(d).wait_send()

    each(0, doms, finish_rest)
    for which in range(2):
        for h in range(2):
            core_copy(which, h).wait_send()


def fused(
    features,
    out_grad,
    gcn_weight,
    tile_index,
    tile_edges,
    halo_rows,
    routes,
    route_weight,
    up_weight,
    down_weight,
):
    doms = lax.axis_size("dom")
    nodes, width = features.shape
    experts, _, units = up_weight.shape
    capacity = capacity_of(nodes, routes.shape[1], experts * doms)
    border = doms * halo_rows.shape[-1]
    block = experts * capacity
    window_rows = 4 * doms * 24
    bf16 = jnp.bfloat16
    dma = pltpu.SemaphoreType.DMA
    whole = pl.BlockSpec(memory_space=pltpu.VMEM)
    away = pl.BlockSpec(memory_space=pl.ANY)
    outs = pl.pallas_call(
        functools.partial(fused_kernel, doms, capacity),
        out_shape=(
            pltpu.VMEM(features.shape, bf16),
            pltpu.VMEM(up_weight.shape, bf16),
            pltpu.VMEM(down_weight.shape, bf16),
        ),
        in_specs=[
            whole,
            whole,
            away,
            pl.BlockSpec(memory_space=pltpu.SMEM),
            whole,
            whole,
            whole,
            whole,
            away,
            away,
        ],
        out_specs=(whole, whole, whole),
        scratch_shapes=[
            pltpu.VMEM(gcn_weight.shape, bf16),
            pltpu.VMEM(up_weight.shape, bf16),
            pltpu.VMEM(down_weight.shape, bf16),
            pltpu.VMEM((border, width), bf16),
            pltpu.VMEM((nodes + border, width), bf16),
            pltpu.VMEM((2, doms, block, width), bf16),
            pltpu.VMEM((2, 4, doms, block, width), bf16),
            pltpu.VMEM((2, window_rows, width), bf16),
            pltpu.VMEM((2, window_rows, width), bf16),
            pltpu.VMEM((2, window_rows, units), bf16),
            pltpu.VMEM((2, window_rows, units), bf16),
            pltpu.VMEM((4, doms, block, width), bf16),
            pltpu.VMEM((2, doms, block, width), bf16),
            pltpu.VMEM((doms, block, width), bf16),
            pltpu.VMEM((2, doms, block, width), bf16),
            pltpu.VMEM((doms, block, width), bf16),
            pltpu.VMEM((nodes, width), bf16),
            dma((3,)),
            dma((doms,)),
            dma((doms,)),
        ]
        + [dma((2, doms))] * 8
        + [dma((2, 2))] * 2
        + [dma((doms,))] * 4,
        compiler_params=pltpu.CompilerParams(
            collective_id=0, has_side_effects=True, vmem_limit_bytes=50 * 1024 * 1024
        ),
    )(
        features,
        out_grad,
        gcn_weight,
        tile_index,
        tile_edges[0],
        halo_rows[0, 0],
        routes.T,
        route_weight.T,
        up_weight,
        down_weight,
    )
    return flush(*outs)


def flush_kernel(node, up, down, node_out, up_out, down_out, sems):
    pairs = [(node, node_out)]
    for source, target in ((up, up_out), (down, down_out)):
        for e in range(source.shape[0]):
            rows = source.shape[1] // 4
            for f in range(4):
                piece = pl.ds(f * rows, rows)
                pairs.append((source.at[e, piece], target.at[e, piece]))
    copies = [pltpu.make_async_copy(a, b, sems.at[i]) for i, (a, b) in enumerate(pairs)]
    for copy in copies:
        copy.start()
    for copy in copies:
        copy.wait()


def flush(*arrays):
    whole = pl.BlockSpec(memory_space=pltpu.VMEM)
    away = pl.BlockSpec(memory_space=pl.ANY)
    return pl.pallas_call(
        flush_kernel,
        out_shape=tuple(jax.ShapeDtypeStruct(a.shape, a.dtype) for a in arrays),
        in_specs=[whole, whole, whole],
        out_specs=(away, away, away),
        scratch_shapes=[pltpu.SemaphoreType.DMA((1 + 8 * arrays[1].shape[0],))],
        compiler_params=pltpu.CompilerParams(vmem_limit_bytes=12 * 1024 * 1024),
    )(*(pltpu.with_memory_space_constraint(a, pltpu.VMEM) for a in arrays))


def layer(features, out_grad, gcn_weight, tile_index, tile_edges, halo_rows, routes, *rest):
    doms, groups = lax.axis_size("dom"), lax.axis_size("group")
    experts = rest[1].shape[0]
    capacity = capacity_of(features.shape[0], routes.shape[1], experts * doms)
    plain = (
        groups == 4
        and experts == 2
        and routes.shape[1] == 2
        and capacity == 20
        and tile_index.shape[0] == 1
        and features.shape[0] == 128
        and tile_edges.shape[-1] == 128
        and rest[1].shape[1:] == (1024, 1024)
        and experts * doms <= 128
        and halo_rows.shape[-1] % 16 == 0
        and doms * halo_rows.shape[-1] % 128 == 0
        and doms == 8
    )
    body = fused if plain else local
    return body(features, out_grad, gcn_weight, tile_index, tile_edges, halo_rows, routes, *rest)


def solution(mesh):
    in_specs = (
        P(("dom", "group"), None),
        P(("dom", "group"), None),
        P(),
        P(("dom", "group"), None),
        P(("dom", "group"), None, None, None),
        P("dom", "group", None, None),
        P(("dom", "group"), None),
        P(("dom", "group"), None),
        P("dom", None, "group"),
        P("dom", "group", None),
    )
    out_specs = (P(("dom", "group"), None), P("dom", None, "group"), P("dom", "group", None))
    return jax.shard_map(layer, mesh=mesh, in_specs=in_specs, out_specs=out_specs, check_vma=False)
```

```python
import functools

import jax
import jax.numpy as jnp
from jax import lax
from jax.experimental import pallas as pl
from jax.experimental.pallas import tpu as pltpu
from jax.sharding import PartitionSpec as P


def silu_slope(values):
    logistic = jax.nn.sigmoid(values)
    return logistic * (1.0 + values * (1.0 - logistic))


def capacity_of(node_count, top_count, expert_count):
    return max(2, 5 * node_count * top_count // (4 * expert_count))


def slot_table(route_rows, expert_count, capacity):
    flat_ids = route_rows.reshape(-1)
    order = jnp.arange(flat_ids.shape[0], dtype=jnp.int32)
    alike = (flat_ids[:, None] == flat_ids[None, :]) & (order[None, :] < order[:, None])
    within = jnp.sum(alike.astype(jnp.int32), axis=1)
    target = flat_ids * capacity + within
    filler = (
        jnp.zeros((expert_count * capacity,), jnp.int32)
        .at[target]
        .set(jnp.arange(flat_ids.shape[0], dtype=jnp.int32) + 1)
    )
    return (target, filler)


def local(
    features,
    out_grad,
    gcn_weight,
    tile_index,
    tile_edges,
    halo_rows,
    routes,
    route_weight,
    up_weight,
    down_weight,
):
    dom_count = lax.axis_size("dom")
    group_count = lax.axis_size("group")
    node_count, width = features.shape
    tile_rows = tile_edges.shape[-1]
    local_tiles = tile_index.shape[0]
    border_rows = halo_rows.shape[-1]
    expert_local = up_weight.shape[0]
    expert_count = expert_local * dom_count
    top_count = routes.shape[1]
    capacity = capacity_of(node_count, top_count, expert_count)
    send_lists = halo_rows.reshape(-1)
    outgoing = features[send_lists].reshape(dom_count, border_rows, width)
    incoming = lax.all_to_all(outgoing, "dom", split_axis=0, concat_axis=0, tiled=True)
    sources = jnp.concatenate(
        [features, incoming.reshape(dom_count * border_rows, width)], axis=0
    ).reshape(-1, tile_rows, width)
    source_tiles = sources.shape[0]
    listed = (tile_index[:, :, None] == jnp.arange(source_tiles, dtype=jnp.int32)).astype(jnp.int32)
    adjacency = jnp.sum(
        tile_edges[:, :, :, None, :] * listed[:, :, None, :, None], axis=1
    ).reshape(local_tiles, tile_rows, source_tiles * tile_rows)
    summed = features.reshape(local_tiles, tile_rows, width).astype(jnp.float32) + jnp.einsum(
        "tij,jd->tid",
        adjacency.astype(jnp.bfloat16),
        sources.reshape(source_tiles * tile_rows, width),
        preferred_element_type=jnp.float32,
    )
    degree = 1.0 + jnp.sum(tile_edges, axis=(1, 3)).astype(jnp.float32)
    aggregated = (
        (summed / jnp.sqrt(degree)[:, :, None]).reshape(node_count, width).astype(jnp.bfloat16)
    )
    preact = jnp.dot(aggregated, gcn_weight, preferred_element_type=jnp.float32)
    hidden = (features.astype(jnp.float32) + jax.nn.silu(preact)).astype(jnp.bfloat16)
    targets, fillers = slot_table(routes, expert_count, capacity)
    cotangent = (
        (route_weight[:, :, None] * out_grad[:, None, :].astype(jnp.float32))
        .astype(jnp.bfloat16)
        .reshape(-1, width)
    )
    present = (fillers > 0)[:, None]
    source_pair = jnp.maximum(fillers - 1, 0)
    nothing = jnp.zeros((), jnp.bfloat16)
    slot_shape = (dom_count, expert_local * capacity, width)
    send_hidden = jnp.where(present, hidden[source_pair // top_count], nothing).reshape(slot_shape)
    send_cot = jnp.where(present, cotangent[source_pair], nothing).reshape(slot_shape)
    mine_cot = lax.all_to_all(send_cot, "dom", split_axis=0, concat_axis=0, tiled=True)
    token_cot = lax.all_gather(mine_cot[None], "group", axis=0, tiled=True)
    mine_hidden = lax.all_to_all(send_hidden, "dom", split_axis=0, concat_axis=0, tiled=True)
    token_hidden = lax.all_gather(mine_hidden[None], "group", axis=0, tiled=True)
    sender_count = group_count * dom_count
    token_hidden = token_hidden.reshape(sender_count, expert_local, capacity, width)
    token_cot = token_cot.reshape(sender_count, expert_local, capacity, width)
    up_proj = jnp.einsum(
        "secd,edf->secf", token_hidden, up_weight, preferred_element_type=jnp.float32
    )
    active = jax.nn.silu(up_proj).astype(jnp.bfloat16)
    merged = lax.psum_scatter(
        jnp.einsum(
            "secf,efd->secd", active, down_weight, preferred_element_type=jnp.float32
        ).astype(jnp.bfloat16),
        "group",
        scatter_dimension=0,
        tiled=True,
    )
    expert_out = merged.reshape(dom_count, expert_local * capacity, width)
    returned = lax.all_to_all(expert_out, "dom", split_axis=0, concat_axis=0, tiled=True).reshape(
        expert_count * capacity, width
    )
    gathered = returned[targets].reshape(node_count, top_count, width)
    node_out = (
        hidden.astype(jnp.float32)
        + jnp.sum(route_weight[:, :, None] * gathered.astype(jnp.float32), axis=1)
    ).astype(jnp.bfloat16)
    grad_act = jnp.einsum(
        "secd,efd->secf", token_cot, down_weight, preferred_element_type=jnp.float32
    )
    grad_pre = (grad_act * silu_slope(up_proj)).astype(jnp.bfloat16)
    down_grad = jnp.einsum(
        "secf,secd->efd", active, token_cot, preferred_element_type=jnp.float32
    ).astype(jnp.bfloat16)
    up_grad = jnp.einsum(
        "secd,secf->edf", token_hidden, grad_pre, preferred_element_type=jnp.float32
    ).astype(jnp.bfloat16)
    return (node_out, up_grad, down_grad)


def dot(left, right, over=((1,), (0,))):
    return lax.dot_general(left, right, (over, ((), ())), preferred_element_type=jnp.float32)


def fused_kernel(
    doms,
    capacity,
    features_in,
    out_grad_in,
    gcn_weight,
    tile_index_in,
    edges_in,
    halo_rows_in,
    routes_in,
    route_weight_in,
    up_weight,
    down_weight,
    node_out,
    up_grad,
    down_grad,
    features,
    halo_rows,
    routes,
    route_weight,
    out_grad,
    edges,
    tile_index,
    gcn,
    up,
    down,
    halo_send,
    sources,
    send,
    token,
    rows_hidden,
    rows_cot,
    active,
    grad_pre,
    partial,
    from_core,
    from_x,
    total,
    returned,
    hidden,
    raw,
    peer_routes,
    peer_weight,
    peer_send,
    weight_sem,
    halo_ss,
    halo_rs,
    slot_ss,
    slot_rs,
    fx_ss,
    fx_rs,
    fc_ss,
    fc_rs,
    fd_ss,
    fd_rs,
    core_ss,
    core_rs,
    x_ss,
    x_rs,
    ret_ss,
    ret_rs,
    raw_ss,
    raw_rs,
    peer_ss,
    peer_rs,
):
    f32, bf16 = jnp.float32, jnp.bfloat16
    dom, group = lax.axis_index("dom"), lax.axis_index("group")
    chip, core = group // 2, group % 2
    other_core = chip * 2 + (1 - core)
    other_chip = (1 - chip) * 2 + core
    nodes, width = features.shape
    borders = halo_rows.shape[1]
    block = 2 * capacity
    window = 24
    second = block - window
    slots = doms * block
    padded = -(-slots // 128) * 128
    experts = 2 * doms
    hidden_units = up.shape[2]
    half = doms // 2
    side = half * window
    batch = 2 * side
    step = 256

    def partner(d):
        place = 0
        for bit in (1, 2, 4):
            mine, theirs = lax.rem(lax.div(dom, bit), 2), lax.rem(lax.div(d, bit), 2)
            place = place + bit * (mine + theirs - 2 * mine * theirs)
        return place

    def own_border(place):
        return pl.ds(pl.multiple_of(nodes + place * borders, borders), borders)

    def remote(src, dst, ss, rs, **where):
        return pltpu.make_async_remote_copy(
            src_ref=src,
            dst_ref=dst,
            send_sem=ss,
            recv_sem=rs,
            device_id=where,
            device_id_type=pl.DeviceIdType.MESH,
        )

    def each(low, high, body):
        def one(place, carry):
            body(place)
            return carry

        lax.fori_loop(low, high, one, 0)

    def side_of(d):
        return lax.div(d, half)

    def halo_copy(d):
        there = partner(d)
        return remote(
            halo_send.at[pl.ds(pl.multiple_of(there * borders, borders), borders)],
            sources.at[own_border(dom)],
            halo_ss.at[0],
            halo_rs.at[side_of(d)],
            dom=there,
            group=group,
        )

    def halo_all(count, h):
        rows = pl.ds(0, count * borders)
        return remote(
            halo_send.at[rows],
            sources.at[rows],
            halo_ss.at[0],
            halo_rs.at[h],
            dom=dom,
            group=other_core,
        )

    def slot(a, d):
        return remote(
            send.at[a, d],
            token.at[a, 0, d],
            slot_ss.at[a],
            slot_rs.at[a, lax.max(d - half + 1, 0)],
            dom=partner(d),
            group=group,
        )

    def slot_all(a, low, high):
        chunks = pl.ds(low, high - low)
        return remote(
            send.at[a, chunks],
            token.at[a, 0, chunks],
            slot_ss.at[a],
            slot_rs.at[a, 0],
            dom=dom,
            group=other_core,
        )

    def forward(a, low, count, src, dst, to, ss, rs):
        chunks = pl.ds(low, count)
        return remote(token.at[a, src, chunks], token.at[a, dst, chunks], ss, rs, dom=dom, group=to)

    def to_chip(a, d, count=1):
        return forward(
            a, d, count, 0, 2, other_chip, fx_ss.at[a], fx_rs.at[a, d - half]
        )

    def to_core(a, d, count=1):
        return forward(
            a, d, count, 0, 1, other_core, fc_ss.at[a], fc_rs.at[a, side_of(d)]
        )

    def relayed(a, d, count=1):
        return forward(
            a, d, count, 2, 3, other_core, fd_ss.at[a], fd_rs.at[a, side_of(d)]
        )

    def pass_on(a, d):
        slot(a, d).wait_recv()
        to_chip(a, d).start()
        to_core(a, d).start()

    def raw_copy(n):
        source = (out_grad_in, hidden, routes_in, route_weight_in)[n]
        target = (raw.at[0], raw.at[1], peer_routes, peer_weight)[n]
        return remote(source, target, raw_ss.at[n], raw_rs.at[n], dom=dom, group=other_chip)

    def peer_slot(a, d, count=1):
        chunks = pl.ds(d, count)
        return remote(
            peer_send.at[a, chunks],
            token.at[a, 2, chunks],
            peer_ss.at[a],
            peer_rs.at[a],
            dom=partner(d),
            group=group,
        )

    def pass_near(a):
        slot_all(a, 1, half).wait_recv()
        to_core(a, 1, half - 1).start()

    def pass_peer(a):
        peer_slot(a, 1, half - 1).wait_recv()
        relayed(a, 1, half - 1).start()

    def relay(a, d):
        to_chip(a, d).wait_recv()
        relayed(a, d).start()

    def core_copy(which, h):
        return remote(
            partial.at[1 + 2 * which, pl.ds(h * half, half)],
            from_core.at[which, pl.ds(h * half, half)],
            core_ss.at[0],
            core_rs.at[which, h],
            dom=dom,
            group=other_core,
        )

    def x_copy(d):
        return remote(
            total.at[1, d], from_x.at[d], x_ss.at[0], x_rs.at[d], dom=dom, group=other_chip
        )

    def ret_copy(d, count=1):
        chunks = pl.ds(d, count)
        return remote(
            total.at[0, chunks],
            returned.at[chunks],
            ret_ss.at[0],
            ret_rs.at[0],
            dom=partner(d),
            group=group,
        )

    row_of = lax.broadcasted_iota(jnp.int32, (window, 1), 0)
    keep = [
        jnp.where(row_of < capacity, 1.0, 0.0).astype(bf16),
        jnp.where(row_of >= window - capacity, 1.0, 0.0).astype(bf16),
    ]
    early = lax.broadcasted_iota(jnp.int32, (window - second, 1), 0) < capacity - second

    def rows_of(h, c):
        if c is None:
            return pl.ds(2 * h * batch, 2 * batch)
        return pl.ds((2 * h + c) * batch, batch)

    def take(a, h, c):
        target = rows_cot if a == 0 else rows_hidden
        for j in range(2):
            start = (2 * h + c) * batch + j * side
            for e in range(2):
                parts = []
                for k in range(half):
                    values = token[a, 2 * c + j, h * half + k, e * second : e * second + window, :]
                    if a == 0:
                        values = values * keep[e]
                    parts.append(values)
                target[e, start : start + side, :] = jnp.concatenate(parts, axis=0)

    def project(h, c, ready=False):
        rows = rows_of(h, c)

        def units(f):
            columns = pl.ds(pl.multiple_of(f * step, step), step)
            projs = [dot(rows_hidden[e, rows, :], up[e, :, columns]) for e in range(2)]
            for e, proj in enumerate(projs):
                gate = 0.5 + 0.5 * jnp.tanh(0.5 * proj)
                value = proj * gate
                active[e, rows, columns] = value.astype(bf16)
                slope = gate + value * (1.0 - gate)
                if ready:
                    slope = slope * grad_pre[e, rows, columns].astype(f32)
                grad_pre[e, rows, columns] = slope.astype(bf16)

        each(0, hidden_units // step, units)

    def combine(h, c):
        rows = rows_of(h, c)
        chips = (0, 1) if c is None else (c,)

        def outs(f):
            columns = pl.ds(pl.multiple_of(f * step, step), step)
            first = dot(active[0, rows, :], down[0, :, columns])
            last = dot(active[1, rows, :], down[1, :, columns])
            for n in range(len(chips) * 2 * half):
                at = n * window
                cut = at + second
                values = jnp.concatenate(
                    [
                        first[at:cut],
                        jnp.where(early, first[cut : at + window], last[at : at + window - second]),
                        last[at + window - second : at + window],
                    ],
                    axis=0,
                )
                rel = 2 * chips[n // (2 * half)] + n // half % 2
                partial[rel, h * half + n % half, :, columns] = values.astype(bf16)

        each(0, width // step, outs)

    def slopes(h, c, first=False):
        rows = rows_of(h, c)

        def units(f):
            columns = pl.ds(pl.multiple_of(f * step, step), step)
            grads = [dot(rows_cot[e, rows, :], down[e, columns, :], ((1,), (1,))) for e in range(2)]
            for e, grad in enumerate(grads):
                if not first:
                    grad = grad * grad_pre[e, rows, columns].astype(f32)
                grad_pre[e, rows, columns] = grad.astype(bf16)

        each(0, hidden_units // step, units)

    def weight_grads(e, h):
        part = pl.ds(512 * h, 512 - h * (1024 - 4 * batch))

        def blocks(f):
            rows = pl.ds(pl.multiple_of(f * 512, 512), 512)
            down_part = dot(active[e, part, rows], rows_cot[e, part, :], ((0,), (0,)))
            if h == 1:
                down_part = down_part + down_grad[e, rows, :].astype(f32)
            down_grad[e, rows, :] = down_part.astype(bf16)
            up_part = dot(rows_hidden[e, part, rows], grad_pre[e, part, :], ((0,), (0,)))
            if h == 1:
                up_part = up_part + up_grad[e, rows, :].astype(f32)
            up_grad[e, rows, :] = up_part.astype(bf16)

        each(0, width // 512, blocks)

    def send_sum(d):
        total[1, d] = (partial[2, d].astype(f32) + from_core[1, d].astype(f32)).astype(bf16)
        x_copy(d).start()

    def sum_up(d):
        x_copy(d).wait_recv()
        return (
            partial[0, d].astype(f32) + from_core[0, d].astype(f32) + from_x[d].astype(f32)
        ).astype(bf16)

    def send_back(d):
        total[0, d] = sum_up(d)
        ret_copy(d).start()

    loads = [
        pltpu.make_async_copy(source, target, weight_sem.at[n])
        for n, (source, target) in enumerate(
            (
                (features_in, features),
                (halo_rows_in, halo_rows),
                (routes_in, routes),
                (route_weight_in, route_weight),
                (out_grad_in, out_grad),
                (edges_in, edges),
                (tile_index_in, tile_index),
                (gcn_weight, gcn),
                (up_weight, up),
                (down_weight, down),
            )
        )
    ]
    barrier = pltpu.get_barrier_semaphore()
    each(
        1,
        doms,
        lambda d: pl.semaphore_signal(
            barrier,
            inc=1,
            device_id={"dom": partner(d), "group": group},
            device_id_type=pl.DeviceIdType.MESH,
        ),
    )
    for peer in (other_core, other_chip):
        pl.semaphore_signal(
            barrier,
            inc=1,
            device_id={"dom": dom, "group": peer},
            device_id_type=pl.DeviceIdType.MESH,
        )
    for load in loads:
        load.start()
    loads[0].wait()
    loads[1].wait()
    own = features[...]
    node_of = lax.broadcasted_iota(jnp.int32, (nodes, borders), 0)
    picks = jnp.concatenate(
        [jnp.where(node_of == halo_rows[b : b + 1, :], 1.0, 0.0).T for b in range(doms)], axis=0
    ).astype(bf16)
    halo_send[...] = dot(picks, own).astype(bf16)
    pl.semaphore_wait(barrier, doms + 1)
    each(half, doms, lambda d: halo_copy(d).start())
    each(1, half, lambda d: halo_copy(d).start())
    for n in (2, 3, 0):
        raw_copy(n).start()
    sources[own_border(dom), :] = halo_send[
        pl.ds(pl.multiple_of(dom * borders, borders), borders), :
    ]
    for n in range(2, 7):
        loads[n].wait()

    expert_of = lax.broadcasted_iota(jnp.int32, (experts, nodes), 0)
    across = lax.broadcasted_iota(jnp.int32, (nodes, nodes), 0)
    along = lax.broadcasted_iota(jnp.int32, (nodes, nodes), 1)
    earlier = jnp.where(across < along, 1.0, 0.0).astype(bf16)

    def tables(chosen, weight, count):
        named = [jnp.where(expert_of == chosen[k : k + 1, :], 1.0, 0.0) for k in range(2)]
        before = dot((named[0] + named[1]).astype(bf16), earlier)
        slot_row = lax.broadcasted_iota(jnp.int32, (count, nodes), 0).astype(f32)
        found = []
        for k in range(2):
            within = jnp.sum(named[k] * before, axis=0, keepdims=True)
            place = chosen[k : k + 1, :]
            place = ((place >> 1) ^ dom) * 2 + (place & 1)
            found.append(jnp.where(slot_row == place.astype(f32) * capacity + within, 1.0, 0.0))
        gate = jnp.sum(
            found[0] * weight[0:1, :] + found[1] * weight[1:2, :], axis=1, keepdims=True
        )
        return found, (found[0] + found[1]).astype(bf16), gate

    slotted, gather, slot_gate = tables(routes[...], route_weight[...], padded)
    gather, slot_gate = gather[0:slots, :], slot_gate[0:slots, :]
    gates = [
        jnp.sum(jnp.where(across == along, route_weight[k : k + 1, :], 0.0), axis=1, keepdims=True)
        for k in range(2)
    ]

    def fill(a, values):
        for d in range(doms):
            part = values[d * block : (d + 1) * block].astype(bf16)
            send[a, d] = part
            if d == 0:
                token[a, 0, 0] = part

    def fill_peer(a, values):
        for d in range(half):
            part = values[d * block : (d + 1) * block].astype(bf16)
            if d == 0:
                token[a, 2, 0] = part
            else:
                peer_send[a, d] = part

    fill(0, dot(gather, out_grad[...]) * slot_gate)
    to_core(0, 0).start()

    near_tile = 1 + lax.div(dom, half)
    far_tile = 3 - near_tile

    def adjacency(t):
        found = jnp.zeros((nodes, nodes), f32)
        for s in range(edges.shape[0]):
            found = found + edges[s].astype(f32) * jnp.where(tile_index[0, s] == t, 1.0, 0.0)
        return found

    def tile(t):
        return sources[pl.ds(pl.multiple_of(t * nodes, nodes), nodes), :]

    matrix = [adjacency(t) for t in (0, near_tile, far_tile)]
    degree = 1.0 + jnp.sum(matrix[0] + matrix[1] + matrix[2], axis=1, keepdims=True)
    root = jnp.sqrt(degree)
    summed = own.astype(f32) + dot(matrix[0].astype(bf16), own)
    raw_copy(2).wait_recv()
    raw_copy(3).wait_recv()
    _, peer_gather, peer_gate = tables(peer_routes[...], peer_weight[...], half * block)
    raw_copy(0).wait_recv()
    fill_peer(0, dot(peer_gather, raw[0]) * peer_gate)
    relayed(0, 0).start()
    loads[7].wait()
    halo_all(half - 1, 0).wait_recv()
    summed = summed + dot(matrix[1].astype(bf16), tile(near_tile))
    halo_all(half, 1).wait_recv()
    summed = summed + dot(matrix[2].astype(bf16), tile(far_tile))
    aggregated = (summed / root).astype(bf16)
    preact = dot(aggregated, gcn[...])
    hidden[...] = (own.astype(f32) + preact / (1.0 + jnp.exp(-preact))).astype(bf16)
    raw_copy(1).start()
    fill(1, dot(gather, hidden[...]))
    each(1, half, lambda d: slot(1, d).start())
    each(half, half + 2, lambda d: slot(1, d).start())
    to_core(1, 0).start()

    def pass_two(a, d):
        pass_on(a, d)
        slot(a, d + 2).start()

    loads[8].wait()
    loads[9].wait()
    raw_copy(1).wait_recv()
    fill_peer(1, dot(peer_gather, raw[1]))
    relayed(1, 0).start()
    each(1, half, lambda d: peer_slot(1, d).start())
    each(half, half + 2, lambda d: pass_two(1, d))
    pass_near(1)
    to_core(1, 0, half).wait_recv()
    take(1, 0, 0)
    project(0, 0)
    each(half + 2, doms, lambda d: pass_on(1, d))
    each(half, half + 2, lambda d: slot(0, d).start())
    to_core(1, half, half).wait_recv()
    take(1, 1, 0)
    project(1, 0)
    pass_peer(1)
    each(1, half, lambda d: slot(0, d).start())
    each(1, half, lambda d: peer_slot(0, d).start())
    relayed(1, 0, half).wait_recv()
    take(1, 0, 1)
    project(0, 1)
    each(half, doms, lambda d: relay(1, d))
    relayed(1, half, half).wait_recv()
    take(1, 1, 1)
    project(1, 1)
    each(half, half + 2, lambda d: pass_two(0, d))
    combine(1, None)
    core_copy(1, 1).start()
    core_copy(0, 1).start()
    core_copy(1, 1).wait_recv()
    each(half, doms, send_sum)
    combine(0, None)
    core_copy(1, 0).start()
    core_copy(0, 0).start()
    core_copy(0, 1).wait_recv()
    send_back(half)
    core_copy(1, 0).wait_recv()
    each(0, half, send_sum)
    pass_near(0)
    pass_peer(0)
    send_back(half + 1)
    each(half + 2, doms, lambda d: pass_on(0, d))
    to_core(0, 0, half).wait_recv()
    take(0, 0, 0)
    relayed(0, 0, half).wait_recv()
    take(0, 0, 1)
    each(half + 2, doms, send_back)
    slopes(0, None)
    each(half, half + 2, lambda d: relay(0, d))
    to_core(0, half, half).wait_recv()
    take(0, 1, 0)
    slopes(1, 0)
    core_copy(0, 0).wait_recv()
    each(1, half, send_back)
    returned[0] = sum_up(0)
    weight_grads(0, 0)
    each(half + 2, doms, lambda d: relay(0, d))
    weight_grads(1, 0)
    relayed(0, half, half).wait_recv()
    take(0, 1, 1)
    slopes(1, 1)
    weight_grads(0, 1)
    weight_grads(1, 1)

    halo_all(doms - 1, 0).wait_send()
    for a in range(2):
        slot_all(a, 1, doms).wait_send()
        peer_slot(a, 1, half - 1).wait_send()
        to_chip(a, half, half).wait_send()
        to_core(a, 0, doms).wait_send()
        relayed(a, 0, doms).wait_send()
    remote(
        partial.at[pl.ds(0, 2)],
        from_core,
        core_ss.at[0],
        core_rs.at[0, 0],
        dom=dom,
        group=other_core,
    ).wait_send()
    remote(total.at[1], from_x, x_ss.at[0], x_rs.at[0], dom=dom, group=other_chip).wait_send()
    for n in range(4):
        raw_copy(n).wait_send()
    ret_copy(1, doms - 1).wait()
    back = jnp.concatenate([returned[d].astype(f32) for d in range(doms)], axis=0).astype(bf16)
    mixed = jnp.zeros((nodes, width), f32)
    for k in range(2):
        mixed = mixed + gates[k] * dot(slotted[k].T[:, 0:slots].astype(bf16), back)
    node_out[...] = (hidden[...].astype(f32) + mixed).astype(bf16)


def fused(
    features,
    out_grad,
    gcn_weight,
    tile_index,
    tile_edges,
    halo_rows,
    routes,
    route_weight,
    up_weight,
    down_weight,
):
    doms = lax.axis_size("dom")
    nodes, width = features.shape
    experts, _, units = up_weight.shape
    capacity = capacity_of(nodes, routes.shape[1], experts * doms)
    border = doms * halo_rows.shape[-1]
    block = experts * capacity
    window_rows = 4 * doms * 24
    bf16 = jnp.bfloat16
    dma = pltpu.SemaphoreType.DMA
    whole = pl.BlockSpec(memory_space=pltpu.VMEM)
    away = pl.BlockSpec(memory_space=pl.ANY)
    outs = pl.pallas_call(
        functools.partial(fused_kernel, doms, capacity),
        out_shape=(
            pltpu.VMEM(features.shape, bf16),
            pltpu.VMEM(up_weight.shape, bf16),
            pltpu.VMEM(down_weight.shape, bf16),
        ),
        in_specs=[away] * 10,
        out_specs=(whole, whole, whole),
        scratch_shapes=[
            pltpu.VMEM(features.shape, bf16),
            pltpu.VMEM(halo_rows.shape[2:], jnp.int32),
            pltpu.VMEM((2, nodes), jnp.int32),
            pltpu.VMEM((2, nodes), jnp.float32),
            pltpu.VMEM(out_grad.shape, bf16),
            pltpu.VMEM(tile_edges.shape[1:], jnp.int32),
            pltpu.SMEM(tile_index.shape, jnp.int32),
            pltpu.VMEM(gcn_weight.shape, bf16),
            pltpu.VMEM(up_weight.shape, bf16),
            pltpu.VMEM(down_weight.shape, bf16),
            pltpu.VMEM((border, width), bf16),
            pltpu.VMEM((nodes + border, width), bf16),
            pltpu.VMEM((2, doms, block, width), bf16),
            pltpu.VMEM((2, 4, doms, block, width), bf16),
            pltpu.VMEM((2, window_rows, width), bf16),
            pltpu.VMEM((2, window_rows, width), bf16),
            pltpu.VMEM((2, window_rows, units), bf16),
            pltpu.VMEM((2, window_rows, units), bf16),
            pltpu.VMEM((4, doms, block, width), bf16),
            pltpu.VMEM((2, doms, block, width), bf16),
            pltpu.VMEM((doms, block, width), bf16),
            pltpu.VMEM((2, doms, block, width), bf16),
            pltpu.VMEM((doms, block, width), bf16),
            pltpu.VMEM((nodes, width), bf16),
            pltpu.VMEM((2, nodes, width), bf16),
            pltpu.VMEM((2, nodes), jnp.int32),
            pltpu.VMEM((2, nodes), jnp.float32),
            pltpu.VMEM((2, doms // 2, block, width), bf16),
            dma((10,)),
            dma((1,)),
            dma((2,)),
            dma((2,)),
            dma((2, 1 + doms // 2)),
            dma((2,)),
            dma((2, doms // 2)),
            dma((2,)),
            dma((2, 2)),
            dma((2,)),
            dma((2, 2)),
            dma((1,)),
            dma((2, 2)),
            dma((1,)),
            dma((doms,)),
            dma((1,)),
            dma((1,)),
            dma((4,)),
            dma((4,)),
            dma((2,)),
            dma((2,)),
        ],
        compiler_params=pltpu.CompilerParams(
            collective_id=0, has_side_effects=True, vmem_limit_bytes=54 * 1024 * 1024
        ),
    )(
        features,
        out_grad,
        gcn_weight,
        tile_index,
        tile_edges[0],
        halo_rows[0, 0],
        routes.T,
        route_weight.T,
        up_weight,
        down_weight,
    )
    return flush(*outs)


def flush_kernel(node, up, down, node_out, up_out, down_out, sems):
    pairs = [(node, node_out)]
    for source, target in ((up, up_out), (down, down_out)):
        for e in range(source.shape[0]):
            rows = source.shape[1] // 4
            for f in range(4):
                piece = pl.ds(f * rows, rows)
                pairs.append((source.at[e, piece], target.at[e, piece]))
    copies = [pltpu.make_async_copy(a, b, sems.at[i]) for i, (a, b) in enumerate(pairs)]
    for copy in copies:
        copy.start()
    for copy in copies:
        copy.wait()


def flush(*arrays):
    whole = pl.BlockSpec(memory_space=pltpu.VMEM)
    away = pl.BlockSpec(memory_space=pl.ANY)
    return pl.pallas_call(
        flush_kernel,
        out_shape=tuple(jax.ShapeDtypeStruct(a.shape, a.dtype) for a in arrays),
        in_specs=[whole, whole, whole],
        out_specs=(away, away, away),
        scratch_shapes=[pltpu.SemaphoreType.DMA((1 + 8 * arrays[1].shape[0],))],
        compiler_params=pltpu.CompilerParams(vmem_limit_bytes=12 * 1024 * 1024),
    )(*(pltpu.with_memory_space_constraint(a, pltpu.VMEM) for a in arrays))


def layer(features, out_grad, gcn_weight, tile_index, tile_edges, halo_rows, routes, *rest):
    doms, groups = lax.axis_size("dom"), lax.axis_size("group")
    experts = rest[1].shape[0]
    capacity = capacity_of(features.shape[0], routes.shape[1], experts * doms)
    plain = (
        groups == 4
        and experts == 2
        and routes.shape[1] == 2
        and capacity == 20
        and tile_index.shape[0] == 1
        and features.shape[0] == 128
        and tile_edges.shape[-1] == 128
        and rest[1].shape[1:] == (1024, 1024)
        and experts * doms <= 128
        and halo_rows.shape[-1] % 16 == 0
        and doms * halo_rows.shape[-1] % 128 == 0
        and doms == 8
    )
    body = fused if plain else local
    return body(features, out_grad, gcn_weight, tile_index, tile_edges, halo_rows, routes, *rest)


def solution(mesh):
    in_specs = (
        P(("dom", "group"), None),
        P(("dom", "group"), None),
        P(),
        P(("dom", "group"), None),
        P(("dom", "group"), None, None, None),
        P("dom", "group", None, None),
        P(("dom", "group"), None),
        P(("dom", "group"), None),
        P("dom", None, "group"),
        P("dom", "group", None),
    )
    out_specs = (P(("dom", "group"), None), P("dom", None, "group"), P("dom", "group", None))
    return jax.shard_map(layer, mesh=mesh, in_specs=in_specs, out_specs=out_specs, check_vma=False)
```

```python
import functools

import jax
import jax.numpy as jnp
from jax import lax
from jax.experimental import pallas as pl
from jax.experimental.pallas import tpu as pltpu
from jax.sharding import PartitionSpec as P


def silu_slope(values):
    logistic = jax.nn.sigmoid(values)
    return logistic * (1.0 + values * (1.0 - logistic))


def capacity_of(node_count, top_count, expert_count):
    return max(2, 5 * node_count * top_count // (4 * expert_count))


def slot_table(route_rows, expert_count, capacity):
    flat_ids = route_rows.reshape(-1)
    order = jnp.arange(flat_ids.shape[0], dtype=jnp.int32)
    alike = (flat_ids[:, None] == flat_ids[None, :]) & (order[None, :] < order[:, None])
    within = jnp.sum(alike.astype(jnp.int32), axis=1)
    target = flat_ids * capacity + within
    filler = (
        jnp.zeros((expert_count * capacity,), jnp.int32)
        .at[target]
        .set(jnp.arange(flat_ids.shape[0], dtype=jnp.int32) + 1)
    )
    return (target, filler)


def local(
    features,
    out_grad,
    gcn_weight,
    tile_index,
    tile_edges,
    halo_rows,
    routes,
    route_weight,
    up_weight,
    down_weight,
):
    dom_count = lax.axis_size("dom")
    group_count = lax.axis_size("group")
    node_count, width = features.shape
    tile_rows = tile_edges.shape[-1]
    local_tiles = tile_index.shape[0]
    border_rows = halo_rows.shape[-1]
    expert_local = up_weight.shape[0]
    expert_count = expert_local * dom_count
    top_count = routes.shape[1]
    capacity = capacity_of(node_count, top_count, expert_count)
    send_lists = halo_rows.reshape(-1)
    outgoing = features[send_lists].reshape(dom_count, border_rows, width)
    incoming = lax.all_to_all(outgoing, "dom", split_axis=0, concat_axis=0, tiled=True)
    sources = jnp.concatenate(
        [features, incoming.reshape(dom_count * border_rows, width)], axis=0
    ).reshape(-1, tile_rows, width)
    source_tiles = sources.shape[0]
    listed = (tile_index[:, :, None] == jnp.arange(source_tiles, dtype=jnp.int32)).astype(jnp.int32)
    adjacency = jnp.sum(
        tile_edges[:, :, :, None, :] * listed[:, :, None, :, None], axis=1
    ).reshape(local_tiles, tile_rows, source_tiles * tile_rows)
    summed = features.reshape(local_tiles, tile_rows, width).astype(jnp.float32) + jnp.einsum(
        "tij,jd->tid",
        adjacency.astype(jnp.bfloat16),
        sources.reshape(source_tiles * tile_rows, width),
        preferred_element_type=jnp.float32,
    )
    degree = 1.0 + jnp.sum(tile_edges, axis=(1, 3)).astype(jnp.float32)
    aggregated = (
        (summed / jnp.sqrt(degree)[:, :, None]).reshape(node_count, width).astype(jnp.bfloat16)
    )
    preact = jnp.dot(aggregated, gcn_weight, preferred_element_type=jnp.float32)
    hidden = (features.astype(jnp.float32) + jax.nn.silu(preact)).astype(jnp.bfloat16)
    targets, fillers = slot_table(routes, expert_count, capacity)
    cotangent = (
        (route_weight[:, :, None] * out_grad[:, None, :].astype(jnp.float32))
        .astype(jnp.bfloat16)
        .reshape(-1, width)
    )
    present = (fillers > 0)[:, None]
    source_pair = jnp.maximum(fillers - 1, 0)
    nothing = jnp.zeros((), jnp.bfloat16)
    slot_shape = (dom_count, expert_local * capacity, width)
    send_hidden = jnp.where(present, hidden[source_pair // top_count], nothing).reshape(slot_shape)
    send_cot = jnp.where(present, cotangent[source_pair], nothing).reshape(slot_shape)
    mine_cot = lax.all_to_all(send_cot, "dom", split_axis=0, concat_axis=0, tiled=True)
    token_cot = lax.all_gather(mine_cot[None], "group", axis=0, tiled=True)
    mine_hidden = lax.all_to_all(send_hidden, "dom", split_axis=0, concat_axis=0, tiled=True)
    token_hidden = lax.all_gather(mine_hidden[None], "group", axis=0, tiled=True)
    sender_count = group_count * dom_count
    token_hidden = token_hidden.reshape(sender_count, expert_local, capacity, width)
    token_cot = token_cot.reshape(sender_count, expert_local, capacity, width)
    up_proj = jnp.einsum(
        "secd,edf->secf", token_hidden, up_weight, preferred_element_type=jnp.float32
    )
    active = jax.nn.silu(up_proj).astype(jnp.bfloat16)
    merged = lax.psum_scatter(
        jnp.einsum(
            "secf,efd->secd", active, down_weight, preferred_element_type=jnp.float32
        ).astype(jnp.bfloat16),
        "group",
        scatter_dimension=0,
        tiled=True,
    )
    expert_out = merged.reshape(dom_count, expert_local * capacity, width)
    returned = lax.all_to_all(expert_out, "dom", split_axis=0, concat_axis=0, tiled=True).reshape(
        expert_count * capacity, width
    )
    gathered = returned[targets].reshape(node_count, top_count, width)
    node_out = (
        hidden.astype(jnp.float32)
        + jnp.sum(route_weight[:, :, None] * gathered.astype(jnp.float32), axis=1)
    ).astype(jnp.bfloat16)
    grad_act = jnp.einsum(
        "secd,efd->secf", token_cot, down_weight, preferred_element_type=jnp.float32
    )
    grad_pre = (grad_act * silu_slope(up_proj)).astype(jnp.bfloat16)
    down_grad = jnp.einsum(
        "secf,secd->efd", active, token_cot, preferred_element_type=jnp.float32
    ).astype(jnp.bfloat16)
    up_grad = jnp.einsum(
        "secd,secf->edf", token_hidden, grad_pre, preferred_element_type=jnp.float32
    ).astype(jnp.bfloat16)
    return (node_out, up_grad, down_grad)


def dot(left, right, over=((1,), (0,))):
    return lax.dot_general(left, right, (over, ((), ())), preferred_element_type=jnp.float32)


def fused_kernel(
    doms,
    capacity,
    features_in,
    out_grad_in,
    gcn_weight,
    tile_index_in,
    edges_in,
    halo_rows_in,
    routes_in,
    route_weight_in,
    up_weight,
    down_weight,
    node_out,
    up_grad,
    down_grad,
    last_hidden,
    last_cot,
    last_active,
    last_pre,
    features,
    halo_rows,
    routes,
    route_weight,
    out_grad,
    edges,
    tile_index,
    gcn,
    up,
    down,
    halo_send,
    sources,
    send,
    token,
    rows_hidden,
    rows_cot,
    active,
    grad_pre,
    partial,
    from_core,
    from_x,
    total,
    returned,
    hidden,
    raw,
    peer_routes,
    peer_weight,
    peer_send,
    weight_sem,
    halo_ss,
    halo_rs,
    slot_ss,
    slot_rs,
    fx_ss,
    fx_rs,
    fc_ss,
    fc_rs,
    fd_ss,
    fd_rs,
    core_ss,
    core_rs,
    x_ss,
    x_rs,
    ret_ss,
    ret_rs,
    raw_ss,
    raw_rs,
    peer_ss,
    peer_rs,
):
    f32, bf16 = jnp.float32, jnp.bfloat16
    dom, group = lax.axis_index("dom"), lax.axis_index("group")
    chip, core = group // 2, group % 2
    other_core = chip * 2 + (1 - core)
    other_chip = (1 - chip) * 2 + core
    nodes, width = features.shape
    borders = halo_rows.shape[1]
    block = 2 * capacity
    window = 24
    second = block - window
    slots = doms * block
    padded = -(-slots // 128) * 128
    experts = 2 * doms
    hidden_units = up.shape[2]
    half = doms // 2
    side = half * window
    batch = 2 * side
    step = 256

    def partner(d):
        place = 0
        for bit in (1, 2, 4):
            mine, theirs = lax.rem(lax.div(dom, bit), 2), lax.rem(lax.div(d, bit), 2)
            place = place + bit * (mine + theirs - 2 * mine * theirs)
        return place

    def own_border(place):
        return pl.ds(pl.multiple_of(nodes + place * borders, borders), borders)

    def remote(src, dst, ss, rs, **where):
        return pltpu.make_async_remote_copy(
            src_ref=src,
            dst_ref=dst,
            send_sem=ss,
            recv_sem=rs,
            device_id=where,
            device_id_type=pl.DeviceIdType.MESH,
        )

    def each(low, high, body):
        def one(place, carry):
            body(place)
            return carry

        lax.fori_loop(low, high, one, 0)

    def side_of(d):
        return lax.div(d, half)

    def halo_copy(d):
        there = partner(d)
        return remote(
            halo_send.at[pl.ds(pl.multiple_of(there * borders, borders), borders)],
            sources.at[own_border(dom)],
            halo_ss.at[0],
            halo_rs.at[side_of(d)],
            dom=there,
            group=group,
        )

    def halo_all(count, h):
        rows = pl.ds(0, count * borders)
        return remote(
            halo_send.at[rows],
            sources.at[rows],
            halo_ss.at[0],
            halo_rs.at[h],
            dom=dom,
            group=other_core,
        )

    def slot(a, d):
        return remote(
            send.at[a, d],
            token.at[a, 0, d],
            slot_ss.at[a],
            slot_rs.at[a, lax.max(d - half + 1, 0)],
            dom=partner(d),
            group=group,
        )

    def slot_all(a, low, high):
        chunks = pl.ds(low, high - low)
        return remote(
            send.at[a, chunks],
            token.at[a, 0, chunks],
            slot_ss.at[a],
            slot_rs.at[a, 0],
            dom=dom,
            group=other_core,
        )

    def forward(a, low, count, src, dst, to, ss, rs):
        chunks = pl.ds(low, count)
        return remote(token.at[a, src, chunks], token.at[a, dst, chunks], ss, rs, dom=dom, group=to)

    def to_chip(a, d, count=1):
        return forward(
            a, d, count, 0, 2, other_chip, fx_ss.at[a], fx_rs.at[a, lax.max(d - half + 1, 0)]
        )

    def to_core(a, d, count=1):
        return forward(
            a, d, count, 0, 1, other_core, fc_ss.at[a], fc_rs.at[a, side_of(d)]
        )

    def relayed(a, d, count=1):
        return forward(
            a, d, count, 2, 3, other_core, fd_ss.at[a], fd_rs.at[a, side_of(d)]
        )

    def pass_on(a, d):
        slot(a, d).wait_recv()
        to_chip(a, d).start()
        to_core(a, d).start()

    def raw_copy(n):
        source = (out_grad_in, routes_in, route_weight_in)[n]
        target = (raw, peer_routes, peer_weight)[n]
        return remote(source, target, raw_ss.at[n], raw_rs.at[n], dom=dom, group=other_chip)

    def peer_slot(d, count=1):
        chunks = pl.ds(d, count)
        return remote(
            peer_send.at[chunks],
            token.at[0, 2, chunks],
            peer_ss.at[0],
            peer_rs.at[0],
            dom=partner(d),
            group=group,
        )

    def pass_near(a):
        slot_all(a, 1, half).wait_recv()
        if a == 1:
            to_chip(a, 1, half - 1).start()
        to_core(a, 1, half - 1).start()

    def pass_peer():
        peer_slot(1, half - 1).wait_recv()
        relayed(0, 1, half - 1).start()

    def relay(a, d):
        to_chip(a, d).wait_recv()
        relayed(a, d).start()

    def core_copy(which, h):
        return remote(
            partial.at[1 + 2 * which, pl.ds(h * half, half)],
            from_core.at[which, pl.ds(h * half, half)],
            core_ss.at[0],
            core_rs.at[which, h],
            dom=dom,
            group=other_core,
        )

    def x_copy(d):
        return remote(
            total.at[1, d], from_x.at[d], x_ss.at[0], x_rs.at[d], dom=dom, group=other_chip
        )

    def ret_copy(d, count=1):
        chunks = pl.ds(d, count)
        return remote(
            total.at[0, chunks],
            returned.at[chunks],
            ret_ss.at[0],
            ret_rs.at[0],
            dom=partner(d),
            group=group,
        )

    row_of = lax.broadcasted_iota(jnp.int32, (window, 1), 0)
    keep = [
        jnp.where(row_of < capacity, 1.0, 0.0).astype(bf16),
        jnp.where(row_of >= window - capacity, 1.0, 0.0).astype(bf16),
    ]
    early = lax.broadcasted_iota(jnp.int32, (window - second, 1), 0) < capacity - second

    def place_of(h, c):
        if h == 1 and c == 1:
            return (last_cot, last_hidden, last_active, last_pre), pl.ds(0, batch)
        count = 2 * batch if c is None else batch
        return (rows_cot, rows_hidden, active, grad_pre), pl.ds((2 * h + (c or 0)) * batch, count)

    def take(a, h, c):
        arrays, rows = place_of(h, c)
        for j in range(2):
            start = rows.start + j * side
            for e in range(2):
                parts = []
                for k in range(half):
                    values = token[a, 2 * c + j, h * half + k, e * second : e * second + window, :]
                    if a == 0:
                        values = values * keep[e]
                    parts.append(values)
                arrays[a][e, start : start + side, :] = jnp.concatenate(parts, axis=0)

    def project(h, c, ready=False):
        (_, hidden_of, active_of, pre_of), rows = place_of(h, c)

        def units(f):
            columns = pl.ds(pl.multiple_of(f * step, step), step)
            projs = [dot(hidden_of[e, rows, :], up[e, :, columns]) for e in range(2)]
            for e, proj in enumerate(projs):
                gate = 0.5 + 0.5 * jnp.tanh(0.5 * proj)
                value = proj * gate
                active_of[e, rows, columns] = value.astype(bf16)
                slope = gate + value * (1.0 - gate)
                if ready:
                    slope = slope * pre_of[e, rows, columns].astype(f32)
                pre_of[e, rows, columns] = slope.astype(bf16)

        each(0, hidden_units // step, units)

    def combine(h, c):
        (_, _, active_of, _), rows = place_of(h, c)
        chips = (0, 1) if c is None else (c,)

        def outs(f):
            columns = pl.ds(pl.multiple_of(f * step, step), step)
            first = dot(active_of[0, rows, :], down[0, :, columns])
            last = dot(active_of[1, rows, :], down[1, :, columns])
            for n in range(len(chips) * 2 * half):
                at = n * window
                cut = at + second
                values = jnp.concatenate(
                    [
                        first[at:cut],
                        jnp.where(early, first[cut : at + window], last[at : at + window - second]),
                        last[at + window - second : at + window],
                    ],
                    axis=0,
                )
                rel = 2 * chips[n // (2 * half)] + n // half % 2
                partial[rel, h * half + n % half, :, columns] = values.astype(bf16)

        each(0, width // step, outs)

    def slopes(h, c, first=False):
        (cot_of, _, _, pre_of), rows = place_of(h, c)

        def units(f):
            columns = pl.ds(pl.multiple_of(f * step, step), step)
            grads = [dot(cot_of[e, rows, :], down[e, columns, :], ((1,), (1,))) for e in range(2)]
            for e, grad in enumerate(grads):
                if not first:
                    grad = grad * pre_of[e, rows, columns].astype(f32)
                pre_of[e, rows, columns] = grad.astype(bf16)

        each(0, hidden_units // step, units)

    def weight_grads(e):
        def blocks(f):
            rows = pl.ds(pl.multiple_of(f * 512, 512), 512)
            down_grad[e, rows, :] = dot(active[e, :, rows], rows_cot[e], ((0,), (0,))).astype(bf16)
            up_grad[e, rows, :] = dot(rows_hidden[e, :, rows], grad_pre[e], ((0,), (0,))).astype(bf16)

        each(0, width // 512, blocks)

    def send_sum(d):
        total[1, d] = (partial[2, d].astype(f32) + from_core[1, d].astype(f32)).astype(bf16)
        x_copy(d).start()

    def sum_up(d):
        x_copy(d).wait_recv()
        return (
            partial[0, d].astype(f32) + from_core[0, d].astype(f32) + from_x[d].astype(f32)
        ).astype(bf16)

    def send_back(d):
        total[0, d] = sum_up(d)
        ret_copy(d).start()

    loads = [
        pltpu.make_async_copy(source, target, weight_sem.at[n])
        for n, (source, target) in enumerate(
            (
                (features_in, features),
                (halo_rows_in, halo_rows),
                (routes_in, routes),
                (route_weight_in, route_weight),
                (out_grad_in, out_grad),
                (edges_in, edges),
                (tile_index_in, tile_index),
                (gcn_weight, gcn),
                (up_weight, up),
                (down_weight, down),
            )
        )
    ]
    barrier = pltpu.get_barrier_semaphore()
    each(
        1,
        doms,
        lambda d: pl.semaphore_signal(
            barrier,
            inc=1,
            device_id={"dom": partner(d), "group": group},
            device_id_type=pl.DeviceIdType.MESH,
        ),
    )
    for peer in (other_core, other_chip):
        pl.semaphore_signal(
            barrier,
            inc=1,
            device_id={"dom": dom, "group": peer},
            device_id_type=pl.DeviceIdType.MESH,
        )
    for load in loads:
        load.start()
    loads[0].wait()
    loads[1].wait()
    own = features[...]
    node_of = lax.broadcasted_iota(jnp.int32, (nodes, borders), 0)
    picks = jnp.concatenate(
        [jnp.where(node_of == halo_rows[b : b + 1, :], 1.0, 0.0).T for b in range(doms)], axis=0
    ).astype(bf16)
    halo_send[...] = dot(picks, own).astype(bf16)
    pl.semaphore_wait(barrier, doms + 1)
    each(half, doms, lambda d: halo_copy(d).start())
    each(1, half, lambda d: halo_copy(d).start())
    for n in (1, 2, 0):
        raw_copy(n).start()
    sources[own_border(dom), :] = halo_send[
        pl.ds(pl.multiple_of(dom * borders, borders), borders), :
    ]
    for n in range(2, 7):
        loads[n].wait()

    expert_of = lax.broadcasted_iota(jnp.int32, (experts, nodes), 0)
    across = lax.broadcasted_iota(jnp.int32, (nodes, nodes), 0)
    along = lax.broadcasted_iota(jnp.int32, (nodes, nodes), 1)
    earlier = jnp.where(across < along, 1.0, 0.0).astype(bf16)

    def tables(chosen, weight, count):
        named = [jnp.where(expert_of == chosen[k : k + 1, :], 1.0, 0.0) for k in range(2)]
        before = dot((named[0] + named[1]).astype(bf16), earlier)
        slot_row = lax.broadcasted_iota(jnp.int32, (count, nodes), 0).astype(f32)
        found = []
        for k in range(2):
            within = jnp.sum(named[k] * before, axis=0, keepdims=True)
            place = chosen[k : k + 1, :]
            place = ((place >> 1) ^ dom) * 2 + (place & 1)
            found.append(jnp.where(slot_row == place.astype(f32) * capacity + within, 1.0, 0.0))
        gate = jnp.sum(
            found[0] * weight[0:1, :] + found[1] * weight[1:2, :], axis=1, keepdims=True
        )
        return found, (found[0] + found[1]).astype(bf16), gate

    slotted, gather, slot_gate = tables(routes[...], route_weight[...], padded)
    gather, slot_gate = gather[0:slots, :], slot_gate[0:slots, :]
    gates = [
        jnp.sum(jnp.where(across == along, route_weight[k : k + 1, :], 0.0), axis=1, keepdims=True)
        for k in range(2)
    ]

    def fill(a, values):
        for d in range(doms):
            part = values[d * block : (d + 1) * block].astype(bf16)
            send[a, d] = part
            if d == 0:
                token[a, 0, 0] = part

    def fill_peer(values):
        for d in range(half):
            part = values[d * block : (d + 1) * block].astype(bf16)
            if d == 0:
                token[0, 2, 0] = part
            else:
                peer_send[d] = part

    fill(0, dot(gather, out_grad[...]) * slot_gate)
    to_core(0, 0).start()

    near_tile = 1 + lax.div(dom, half)
    far_tile = 3 - near_tile

    def adjacency(t):
        found = jnp.zeros((nodes, nodes), f32)
        for s in range(edges.shape[0]):
            found = found + edges[s].astype(f32) * jnp.where(tile_index[0, s] == t, 1.0, 0.0)
        return found

    def tile(t):
        return sources[pl.ds(pl.multiple_of(t * nodes, nodes), nodes), :]

    matrix = [adjacency(t) for t in (0, near_tile, far_tile)]
    degree = 1.0 + jnp.sum(matrix[0] + matrix[1] + matrix[2], axis=1, keepdims=True)
    root = jnp.sqrt(degree)
    summed = own.astype(f32) + dot(matrix[0].astype(bf16), own)
    raw_copy(1).wait_recv()
    raw_copy(2).wait_recv()
    _, peer_gather, peer_gate = tables(peer_routes[...], peer_weight[...], half * block)
    raw_copy(0).wait_recv()
    fill_peer(dot(peer_gather, raw[...]) * peer_gate)
    relayed(0, 0).start()
    each(1, half, lambda d: slot(0, d).start())
    each(1, half, lambda d: peer_slot(d).start())
    loads[7].wait()
    halo_all(half - 1, 0).wait_recv()
    summed = summed + dot(matrix[1].astype(bf16), tile(near_tile))
    halo_all(half, 1).wait_recv()
    summed = summed + dot(matrix[2].astype(bf16), tile(far_tile))
    aggregated = (summed / root).astype(bf16)
    preact = dot(aggregated, gcn[...])
    hidden[...] = (own.astype(f32) + preact / (1.0 + jnp.exp(-preact))).astype(bf16)
    fill(1, dot(gather, hidden[...]))
    each(1, half, lambda d: slot(1, d).start())
    each(half, half + 2, lambda d: slot(1, d).start())
    to_chip(1, 0).start()
    to_core(1, 0).start()

    def pass_two(a, d):
        pass_on(a, d)
        slot(a, d + 2).start()

    loads[8].wait()
    loads[9].wait()
    each(half, half + 2, lambda d: pass_two(1, d))
    pass_near(1)
    pass_near(0)
    pass_peer()
    to_core(0, 0, half).wait_recv()
    take(0, 0, 0)
    relayed(0, 0, half).wait_recv()
    take(0, 0, 1)
    slopes(0, None, True)
    to_core(1, 0, half).wait_recv()
    take(1, 0, 0)
    each(half + 2, doms, lambda d: pass_on(1, d))
    project(0, 0, True)
    each(half, doms, lambda d: slot(0, d).start())
    to_chip(1, 0, half).wait_recv()
    relayed(1, 0, half).start()
    relayed(1, 0, half).wait_recv()
    take(1, 0, 1)
    project(0, 1, True)
    each(half, half + 2, lambda d: relay(1, d))
    combine(0, 1)
    core_copy(1, 0).start()
    each(half + 2, doms, lambda d: relay(1, d))
    to_core(1, half, half).wait_recv()
    take(1, 1, 0)
    project(1, 0)
    core_copy(1, 0).wait_recv()
    each(0, half, send_sum)
    relayed(1, half, half).wait_recv()
    take(1, 1, 1)
    project(1, 1)
    combine(1, 1)
    core_copy(1, 1).start()
    combine(0, 0)
    core_copy(0, 0).start()
    core_copy(1, 1).wait_recv()
    each(half, doms, send_sum)
    combine(1, 0)
    core_copy(0, 1).start()
    each(half, doms, lambda d: pass_on(0, d))
    core_copy(0, 0).wait_recv()
    each(1, half, send_back)
    returned[0] = sum_up(0)
    to_core(0, half, half).wait_recv()
    take(0, 1, 0)
    slopes(1, 0)
    core_copy(0, 1).wait_recv()
    each(half, half + 2, send_back)
    weight_grads(0)
    each(half + 2, doms, send_back)
    weight_grads(1)
    each(half, doms, lambda d: relay(0, d))
    relayed(0, half, half).wait_recv()
    take(0, 1, 1)
    slopes(1, 1)

    halo_all(doms - 1, 0).wait_send()
    for a in range(2):
        slot_all(a, 1, doms).wait_send()
        if a == 0:
            peer_slot(1, half - 1).wait_send()
            to_chip(a, half, half).wait_send()
        else:
            to_chip(a, 0, doms).wait_send()
        to_core(a, 0, doms).wait_send()
        relayed(a, 0, doms).wait_send()
    remote(
        partial.at[pl.ds(0, 2)],
        from_core,
        core_ss.at[0],
        core_rs.at[0, 0],
        dom=dom,
        group=other_core,
    ).wait_send()
    remote(total.at[1], from_x, x_ss.at[0], x_rs.at[0], dom=dom, group=other_chip).wait_send()
    for n in range(3):
        raw_copy(n).wait_send()
    ret_copy(1, doms - 1).wait()
    back = jnp.concatenate([returned[d].astype(f32) for d in range(doms)], axis=0).astype(bf16)
    mixed = jnp.zeros((nodes, width), f32)
    for k in range(2):
        mixed = mixed + gates[k] * dot(slotted[k].T[:, 0:slots].astype(bf16), back)
    node_out[...] = (hidden[...].astype(f32) + mixed).astype(bf16)


def fused(
    features,
    out_grad,
    gcn_weight,
    tile_index,
    tile_edges,
    halo_rows,
    routes,
    route_weight,
    up_weight,
    down_weight,
):
    doms = lax.axis_size("dom")
    nodes, width = features.shape
    experts, _, units = up_weight.shape
    capacity = capacity_of(nodes, routes.shape[1], experts * doms)
    border = doms * halo_rows.shape[-1]
    block = experts * capacity
    last_rows = doms * 24
    window_rows = 3 * last_rows
    bf16 = jnp.bfloat16
    dma = pltpu.SemaphoreType.DMA
    whole = pl.BlockSpec(memory_space=pltpu.VMEM)
    away = pl.BlockSpec(memory_space=pl.ANY)
    outs = pl.pallas_call(
        functools.partial(fused_kernel, doms, capacity),
        out_shape=(
            pltpu.VMEM(features.shape, bf16),
            pltpu.VMEM(up_weight.shape, bf16),
            pltpu.VMEM(down_weight.shape, bf16),
            *[pltpu.VMEM((experts, last_rows, size), bf16) for size in (width, width, units, units)],
        ),
        in_specs=[away] * 10,
        out_specs=(whole,) * 7,
        scratch_shapes=[
            pltpu.VMEM(features.shape, bf16),
            pltpu.VMEM(halo_rows.shape[2:], jnp.int32),
            pltpu.VMEM((2, nodes), jnp.int32),
            pltpu.VMEM((2, nodes), jnp.float32),
            pltpu.VMEM(out_grad.shape, bf16),
            pltpu.VMEM(tile_edges.shape[1:], jnp.int32),
            pltpu.SMEM(tile_index.shape, jnp.int32),
            pltpu.VMEM(gcn_weight.shape, bf16),
            pltpu.VMEM(up_weight.shape, bf16),
            pltpu.VMEM(down_weight.shape, bf16),
            pltpu.VMEM((border, width), bf16),
            pltpu.VMEM((nodes + border, width), bf16),
            pltpu.VMEM((2, doms, block, width), bf16),
            pltpu.VMEM((2, 4, doms, block, width), bf16),
            pltpu.VMEM((2, window_rows, width), bf16),
            pltpu.VMEM((2, window_rows, width), bf16),
            pltpu.VMEM((2, window_rows, units), bf16),
            pltpu.VMEM((2, window_rows, units), bf16),
            pltpu.VMEM((4, doms, block, width), bf16),
            pltpu.VMEM((2, doms, block, width), bf16),
            pltpu.VMEM((doms, block, width), bf16),
            pltpu.VMEM((2, doms, block, width), bf16),
            pltpu.VMEM((doms, block, width), bf16),
            pltpu.VMEM((nodes, width), bf16),
            pltpu.VMEM((nodes, width), bf16),
            pltpu.VMEM((2, nodes), jnp.int32),
            pltpu.VMEM((2, nodes), jnp.float32),
            pltpu.VMEM((doms // 2, block, width), bf16),
            dma((10,)),
            dma((1,)),
            dma((2,)),
            dma((2,)),
            dma((2, 1 + doms // 2)),
            dma((2,)),
            dma((2, 1 + doms // 2)),
            dma((2,)),
            dma((2, 2)),
            dma((2,)),
            dma((2, 2)),
            dma((1,)),
            dma((2, 2)),
            dma((1,)),
            dma((doms,)),
            dma((1,)),
            dma((1,)),
            dma((3,)),
            dma((3,)),
            dma((1,)),
            dma((1,)),
        ],
        compiler_params=pltpu.CompilerParams(
            collective_id=0, has_side_effects=True, vmem_limit_bytes=44 * 1024 * 1024
        ),
    )(
        features,
        out_grad,
        gcn_weight,
        tile_index,
        tile_edges[0],
        halo_rows[0, 0],
        routes.T,
        route_weight.T,
        up_weight,
        down_weight,
    )
    return finish(*outs)


def finish_kernel(
    node, up, down, hidden, cot, active, pre, node_out, up_out, down_out, up_sum, down_sum, sems
):
    experts, width, _ = up.shape
    rows = width // 2
    copies = [pltpu.make_async_copy(node, node_out, sems.at[0])]
    copies[0].start()
    parts = ((active, cot, down, down_sum, down_out), (hidden, pre, up, up_sum, up_out))
    for e in range(experts):
        for f in range(2):
            piece = pl.ds(f * rows, rows)
            for left, right, part, total, out in parts:
                added = dot(left[e, :, piece], right[e], ((0,), (0,)))
                total[e, piece, :] = (part[e, piece, :].astype(jnp.float32) + added).astype(out.dtype)
                copy = pltpu.make_async_copy(
                    total.at[e, piece], out.at[e, piece], sems.at[len(copies)]
                )
                copy.start()
                copies.append(copy)
    for copy in copies:
        copy.wait()


def finish(*arrays):
    whole = pl.BlockSpec(memory_space=pltpu.VMEM)
    away = pl.BlockSpec(memory_space=pl.ANY)
    results = arrays[:3]
    return pl.pallas_call(
        finish_kernel,
        out_shape=tuple(jax.ShapeDtypeStruct(a.shape, a.dtype) for a in results),
        in_specs=[whole] * 7,
        out_specs=(away, away, away),
        scratch_shapes=[
            pltpu.VMEM(arrays[1].shape, arrays[1].dtype),
            pltpu.VMEM(arrays[2].shape, arrays[2].dtype),
            pltpu.SemaphoreType.DMA((1 + 4 * arrays[1].shape[0],)),
        ],
        compiler_params=pltpu.CompilerParams(vmem_limit_bytes=24 * 1024 * 1024),
    )(*(pltpu.with_memory_space_constraint(a, pltpu.VMEM) for a in arrays))


def layer(features, out_grad, gcn_weight, tile_index, tile_edges, halo_rows, routes, *rest):
    doms, groups = lax.axis_size("dom"), lax.axis_size("group")
    experts = rest[1].shape[0]
    capacity = capacity_of(features.shape[0], routes.shape[1], experts * doms)
    plain = (
        groups == 4
        and experts == 2
        and routes.shape[1] == 2
        and capacity == 20
        and tile_index.shape[0] == 1
        and features.shape[0] == 128
        and tile_edges.shape[-1] == 128
        and rest[1].shape[1:] == (1024, 1024)
        and experts * doms <= 128
        and halo_rows.shape[-1] % 16 == 0
        and doms * halo_rows.shape[-1] % 128 == 0
        and doms == 8
    )
    body = fused if plain else local
    return body(features, out_grad, gcn_weight, tile_index, tile_edges, halo_rows, routes, *rest)


def solution(mesh):
    in_specs = (
        P(("dom", "group"), None),
        P(("dom", "group"), None),
        P(),
        P(("dom", "group"), None),
        P(("dom", "group"), None, None, None),
        P("dom", "group", None, None),
        P(("dom", "group"), None),
        P(("dom", "group"), None),
        P("dom", None, "group"),
        P("dom", "group", None),
    )
    out_specs = (P(("dom", "group"), None), P("dom", None, "group"), P("dom", "group", None))
    return jax.shard_map(layer, mesh=mesh, in_specs=in_specs, out_specs=out_specs, check_vma=False)
```

```python
import functools

import jax
import jax.numpy as jnp
from jax import lax
from jax.experimental import pallas as pl
from jax.experimental.pallas import tpu as pltpu
from jax.sharding import PartitionSpec as P


def silu_slope(values):
    logistic = jax.nn.sigmoid(values)
    return logistic * (1.0 + values * (1.0 - logistic))


def capacity_of(node_count, top_count, expert_count):
    return max(2, 5 * node_count * top_count // (4 * expert_count))


def slot_table(route_rows, expert_count, capacity):
    flat_ids = route_rows.reshape(-1)
    order = jnp.arange(flat_ids.shape[0], dtype=jnp.int32)
    alike = (flat_ids[:, None] == flat_ids[None, :]) & (order[None, :] < order[:, None])
    within = jnp.sum(alike.astype(jnp.int32), axis=1)
    target = flat_ids * capacity + within
    filler = (
        jnp.zeros((expert_count * capacity,), jnp.int32)
        .at[target]
        .set(jnp.arange(flat_ids.shape[0], dtype=jnp.int32) + 1)
    )
    return (target, filler)


def local(
    features,
    out_grad,
    gcn_weight,
    tile_index,
    tile_edges,
    halo_rows,
    routes,
    route_weight,
    up_weight,
    down_weight,
):
    dom_count = lax.axis_size("dom")
    group_count = lax.axis_size("group")
    node_count, width = features.shape
    tile_rows = tile_edges.shape[-1]
    local_tiles = tile_index.shape[0]
    border_rows = halo_rows.shape[-1]
    expert_local = up_weight.shape[0]
    expert_count = expert_local * dom_count
    top_count = routes.shape[1]
    capacity = capacity_of(node_count, top_count, expert_count)
    send_lists = halo_rows.reshape(-1)
    outgoing = features[send_lists].reshape(dom_count, border_rows, width)
    incoming = lax.all_to_all(outgoing, "dom", split_axis=0, concat_axis=0, tiled=True)
    sources = jnp.concatenate(
        [features, incoming.reshape(dom_count * border_rows, width)], axis=0
    ).reshape(-1, tile_rows, width)
    source_tiles = sources.shape[0]
    listed = (tile_index[:, :, None] == jnp.arange(source_tiles, dtype=jnp.int32)).astype(jnp.int32)
    adjacency = jnp.sum(
        tile_edges[:, :, :, None, :] * listed[:, :, None, :, None], axis=1
    ).reshape(local_tiles, tile_rows, source_tiles * tile_rows)
    summed = features.reshape(local_tiles, tile_rows, width).astype(jnp.float32) + jnp.einsum(
        "tij,jd->tid",
        adjacency.astype(jnp.bfloat16),
        sources.reshape(source_tiles * tile_rows, width),
        preferred_element_type=jnp.float32,
    )
    degree = 1.0 + jnp.sum(tile_edges, axis=(1, 3)).astype(jnp.float32)
    aggregated = (
        (summed / jnp.sqrt(degree)[:, :, None]).reshape(node_count, width).astype(jnp.bfloat16)
    )
    preact = jnp.dot(aggregated, gcn_weight, preferred_element_type=jnp.float32)
    hidden = (features.astype(jnp.float32) + jax.nn.silu(preact)).astype(jnp.bfloat16)
    targets, fillers = slot_table(routes, expert_count, capacity)
    cotangent = (
        (route_weight[:, :, None] * out_grad[:, None, :].astype(jnp.float32))
        .astype(jnp.bfloat16)
        .reshape(-1, width)
    )
    present = (fillers > 0)[:, None]
    source_pair = jnp.maximum(fillers - 1, 0)
    nothing = jnp.zeros((), jnp.bfloat16)
    slot_shape = (dom_count, expert_local * capacity, width)
    send_hidden = jnp.where(present, hidden[source_pair // top_count], nothing).reshape(slot_shape)
    send_cot = jnp.where(present, cotangent[source_pair], nothing).reshape(slot_shape)
    mine_cot = lax.all_to_all(send_cot, "dom", split_axis=0, concat_axis=0, tiled=True)
    token_cot = lax.all_gather(mine_cot[None], "group", axis=0, tiled=True)
    mine_hidden = lax.all_to_all(send_hidden, "dom", split_axis=0, concat_axis=0, tiled=True)
    token_hidden = lax.all_gather(mine_hidden[None], "group", axis=0, tiled=True)
    sender_count = group_count * dom_count
    token_hidden = token_hidden.reshape(sender_count, expert_local, capacity, width)
    token_cot = token_cot.reshape(sender_count, expert_local, capacity, width)
    up_proj = jnp.einsum(
        "secd,edf->secf", token_hidden, up_weight, preferred_element_type=jnp.float32
    )
    active = jax.nn.silu(up_proj).astype(jnp.bfloat16)
    merged = lax.psum_scatter(
        jnp.einsum(
            "secf,efd->secd", active, down_weight, preferred_element_type=jnp.float32
        ).astype(jnp.bfloat16),
        "group",
        scatter_dimension=0,
        tiled=True,
    )
    expert_out = merged.reshape(dom_count, expert_local * capacity, width)
    returned = lax.all_to_all(expert_out, "dom", split_axis=0, concat_axis=0, tiled=True).reshape(
        expert_count * capacity, width
    )
    gathered = returned[targets].reshape(node_count, top_count, width)
    node_out = (
        hidden.astype(jnp.float32)
        + jnp.sum(route_weight[:, :, None] * gathered.astype(jnp.float32), axis=1)
    ).astype(jnp.bfloat16)
    grad_act = jnp.einsum(
        "secd,efd->secf", token_cot, down_weight, preferred_element_type=jnp.float32
    )
    grad_pre = (grad_act * silu_slope(up_proj)).astype(jnp.bfloat16)
    down_grad = jnp.einsum(
        "secf,secd->efd", active, token_cot, preferred_element_type=jnp.float32
    ).astype(jnp.bfloat16)
    up_grad = jnp.einsum(
        "secd,secf->edf", token_hidden, grad_pre, preferred_element_type=jnp.float32
    ).astype(jnp.bfloat16)
    return (node_out, up_grad, down_grad)


def dot(left, right, over=((1,), (0,))):
    return lax.dot_general(left, right, (over, ((), ())), preferred_element_type=jnp.float32)


def fused_kernel(
    doms,
    capacity,
    features_in,
    out_grad_in,
    gcn_weight,
    tile_index_in,
    edges_in,
    halo_rows_in,
    routes_in,
    route_weight_in,
    up_weight,
    down_weight,
    node_out,
    up_grad,
    down_grad,
    last_hidden,
    last_cot,
    last_active,
    last_pre,
    features,
    halo_rows,
    routes,
    route_weight,
    out_grad,
    edges,
    tile_index,
    gcn,
    up,
    down,
    halo_send,
    sources,
    send,
    token,
    rows_hidden,
    rows_cot,
    active,
    grad_pre,
    partial,
    from_core,
    from_x,
    total,
    returned,
    hidden,
    raw,
    peer_routes,
    peer_weight,
    peer_send,
    weight_sem,
    halo_ss,
    halo_rs,
    slot_ss,
    slot_rs,
    fx_ss,
    fx_rs,
    fc_ss,
    fc_rs,
    fd_ss,
    fd_rs,
    core_ss,
    core_rs,
    x_ss,
    x_rs,
    ret_ss,
    ret_rs,
    raw_ss,
    raw_rs,
    peer_ss,
    peer_rs,
):
    f32, bf16 = jnp.float32, jnp.bfloat16
    dom, group = lax.axis_index("dom"), lax.axis_index("group")
    chip, core = group // 2, group % 2
    other_core = chip * 2 + (1 - core)
    other_chip = (1 - chip) * 2 + core
    nodes, width = features.shape
    borders = halo_rows.shape[1]
    block = 2 * capacity
    window = 24
    second = block - window
    slots = doms * block
    padded = -(-slots // 128) * 128
    experts = 2 * doms
    hidden_units = up.shape[2]
    half = doms // 2
    side = half * window
    batch = 2 * side
    step = 256

    def partner(d):
        place = 0
        for bit in (1, 2, 4):
            mine, theirs = lax.rem(lax.div(dom, bit), 2), lax.rem(lax.div(d, bit), 2)
            place = place + bit * (mine + theirs - 2 * mine * theirs)
        return place

    def own_border(place):
        return pl.ds(pl.multiple_of(nodes + place * borders, borders), borders)

    def remote(src, dst, ss, rs, **where):
        return pltpu.make_async_remote_copy(
            src_ref=src,
            dst_ref=dst,
            send_sem=ss,
            recv_sem=rs,
            device_id=where,
            device_id_type=pl.DeviceIdType.MESH,
        )

    def each(low, high, body, unroll=1):
        def one(place, carry):
            body(place)
            return carry

        lax.fori_loop(low, high, one, 0, unroll=unroll)

    def side_of(d):
        return lax.div(d, half)

    def halo_copy(d):
        there = partner(d)
        return remote(
            halo_send.at[pl.ds(pl.multiple_of(there * borders, borders), borders)],
            sources.at[own_border(dom)],
            halo_ss.at[0],
            halo_rs.at[side_of(d)],
            dom=there,
            group=group,
        )

    def halo_all(count, h):
        rows = pl.ds(0, count * borders)
        return remote(
            halo_send.at[rows],
            sources.at[rows],
            halo_ss.at[0],
            halo_rs.at[h],
            dom=dom,
            group=other_core,
        )

    def slot(a, d):
        return remote(
            send.at[a, d],
            token.at[a, 0, d],
            slot_ss.at[a],
            slot_rs.at[a, lax.max(d - half + 2, lax.min(d - 1, 1))],
            dom=partner(d),
            group=group,
        )

    def slot_all(a, low, high):
        chunks = pl.ds(low, high - low)
        return remote(
            send.at[a, chunks],
            token.at[a, 0, chunks],
            slot_ss.at[a],
            slot_rs.at[a, 1],
            dom=dom,
            group=other_core,
        )

    def forward(a, low, count, src, dst, to, ss, rs):
        chunks = pl.ds(low, count)
        return remote(token.at[a, src, chunks], token.at[a, dst, chunks], ss, rs, dom=dom, group=to)

    def to_chip(a, d, count=1):
        return forward(
            a, d, count, 0, 2, other_chip, fx_ss.at[a], fx_rs.at[a, lax.max(d - half + 1, 0)]
        )

    def to_core(a, d, count=1):
        return forward(
            a, d, count, 0, 1, other_core, fc_ss.at[a], fc_rs.at[a, side_of(d)]
        )

    def relayed(a, d, count=1):
        return forward(
            a, d, count, 2, 3, other_core, fd_ss.at[a], fd_rs.at[a, side_of(d)]
        )

    def pass_on(a, d):
        slot(a, d).wait_recv()
        to_chip(a, d).start()
        to_core(a, d).start()

    def raw_copy(n):
        source = (out_grad_in, routes_in, route_weight_in)[n]
        target = (raw, peer_routes, peer_weight)[n]
        return remote(source, target, raw_ss.at[n], raw_rs.at[n], dom=dom, group=other_chip)

    def peer_slot(d, count=1):
        chunks = pl.ds(d, count)
        return remote(
            peer_send.at[chunks],
            token.at[0, 2, chunks],
            peer_ss.at[0],
            peer_rs.at[0],
            dom=partner(d),
            group=group,
        )

    def pass_near(a):
        slot_all(a, 2, half).wait_recv()
        if a == 1:
            to_chip(a, 2, half - 2).start()
        to_core(a, 2, half - 2).start()

    def pass_peer():
        peer_slot(1, half - 1).wait_recv()
        relayed(0, 1, half - 1).start()

    def relay(a, d):
        to_chip(a, d).wait_recv()
        relayed(a, d).start()

    def core_copy(which, h):
        return remote(
            partial.at[1 + 2 * which, pl.ds(h * half, half)],
            from_core.at[which, pl.ds(h * half, half)],
            core_ss.at[0],
            core_rs.at[which, h],
            dom=dom,
            group=other_core,
        )

    def x_copy(d):
        return remote(
            total.at[1, d], from_x.at[d], x_ss.at[0], x_rs.at[d], dom=dom, group=other_chip
        )

    def ret_copy(d, count=1):
        chunks = pl.ds(d, count)
        return remote(
            total.at[0, chunks],
            returned.at[chunks],
            ret_ss.at[0],
            ret_rs.at[0],
            dom=partner(d),
            group=group,
        )

    row_of = lax.broadcasted_iota(jnp.int32, (window, 1), 0)
    keep = [
        jnp.where(row_of < capacity, 1.0, 0.0).astype(bf16),
        jnp.where(row_of >= window - capacity, 1.0, 0.0).astype(bf16),
    ]
    early = lax.broadcasted_iota(jnp.int32, (window - second, 1), 0) < capacity - second

    def place_of(h, c):
        if h == 1 and c == 1:
            return (last_cot, last_hidden, last_active, last_pre), pl.ds(0, batch)
        count = 2 * batch if c is None else batch
        return (rows_cot, rows_hidden, active, grad_pre), pl.ds((2 * h + (c or 0)) * batch, count)

    def take(a, h, c):
        arrays, rows = place_of(h, c)
        for j in range(2):
            start = rows.start + j * side
            for e in range(2):
                parts = []
                for k in range(half):
                    values = token[a, 2 * c + j, h * half + k, e * second : e * second + window, :]
                    if a == 0:
                        values = values * keep[e]
                    parts.append(values)
                arrays[a][e, start : start + side, :] = jnp.concatenate(parts, axis=0)

    def project(h, c, ready=False):
        (_, hidden_of, active_of, pre_of), rows = place_of(h, c)

        def units(f):
            columns = pl.ds(pl.multiple_of(f * step, step), step)
            projs = [dot(hidden_of[e, rows, :], up[e, :, columns]) for e in range(2)]
            for e, proj in enumerate(projs):
                gate = 0.5 + 0.5 * jnp.tanh(0.5 * proj)
                value = proj * gate
                active_of[e, rows, columns] = value.astype(bf16)
                slope = gate + value * (1.0 - gate)
                if ready:
                    slope = slope * pre_of[e, rows, columns].astype(f32)
                pre_of[e, rows, columns] = slope.astype(bf16)

        each(0, hidden_units // step, units, 2)

    def combine(h, c):
        (_, _, active_of, _), rows = place_of(h, c)
        chips = (0, 1) if c is None else (c,)

        def outs(f):
            columns = pl.ds(pl.multiple_of(f * step, step), step)
            first = dot(active_of[0, rows, :], down[0, :, columns])
            last = dot(active_of[1, rows, :], down[1, :, columns])
            for n in range(len(chips) * 2 * half):
                at = n * window
                cut = at + second
                values = jnp.concatenate(
                    [
                        first[at:cut],
                        jnp.where(early, first[cut : at + window], last[at : at + window - second]),
                        last[at + window - second : at + window],
                    ],
                    axis=0,
                )
                rel = 2 * chips[n // (2 * half)] + n // half % 2
                partial[rel, h * half + n % half, :, columns] = values.astype(bf16)

        each(0, width // step, outs, 2)

    def slopes(h, c, first=False):
        (cot_of, _, _, pre_of), rows = place_of(h, c)

        def units(f):
            columns = pl.ds(pl.multiple_of(f * step, step), step)
            grads = [dot(cot_of[e, rows, :], down[e, columns, :], ((1,), (1,))) for e in range(2)]
            for e, grad in enumerate(grads):
                if not first:
                    grad = grad * pre_of[e, rows, columns].astype(f32)
                pre_of[e, rows, columns] = grad.astype(bf16)

        each(0, hidden_units // step, units, 2)

    def weight_grads(e):
        def blocks(f):
            rows = pl.ds(pl.multiple_of(f * 512, 512), 512)
            down_grad[e, rows, :] = dot(active[e, :, rows], rows_cot[e], ((0,), (0,))).astype(bf16)
            up_grad[e, rows, :] = dot(rows_hidden[e, :, rows], grad_pre[e], ((0,), (0,))).astype(bf16)

        each(0, width // 512, blocks)

    def send_sum(d):
        total[1, d] = (partial[2, d].astype(f32) + from_core[1, d].astype(f32)).astype(bf16)
        x_copy(d).start()

    def sum_up(d):
        x_copy(d).wait_recv()
        return (
            partial[0, d].astype(f32) + from_core[0, d].astype(f32) + from_x[d].astype(f32)
        ).astype(bf16)

    def send_back(d):
        total[0, d] = sum_up(d)
        ret_copy(d).start()

    loads = [
        pltpu.make_async_copy(source, target, weight_sem.at[n])
        for n, (source, target) in enumerate(
            (
                (features_in, features),
                (halo_rows_in, halo_rows),
                (routes_in, routes),
                (route_weight_in, route_weight),
                (out_grad_in, out_grad),
                (edges_in, edges),
                (tile_index_in, tile_index),
                (gcn_weight, gcn),
                (up_weight, up),
                (down_weight, down),
            )
        )
    ]
    barrier = pltpu.get_barrier_semaphore()
    each(
        1,
        doms,
        lambda d: pl.semaphore_signal(
            barrier,
            inc=1,
            device_id={"dom": partner(d), "group": group},
            device_id_type=pl.DeviceIdType.MESH,
        ),
    )
    for peer in (other_core, other_chip):
        pl.semaphore_signal(
            barrier,
            inc=1,
            device_id={"dom": dom, "group": peer},
            device_id_type=pl.DeviceIdType.MESH,
        )
    for load in loads:
        load.start()
    loads[0].wait()
    loads[1].wait()
    own = features[...]
    node_of = lax.broadcasted_iota(jnp.int32, (nodes, borders), 0)
    picks = jnp.concatenate(
        [jnp.where(node_of == halo_rows[b : b + 1, :], 1.0, 0.0).T for b in range(doms)], axis=0
    ).astype(bf16)
    halo_send[...] = dot(picks, own).astype(bf16)
    pl.semaphore_wait(barrier, doms + 1)
    each(half, doms, lambda d: halo_copy(d).start())
    each(1, half, lambda d: halo_copy(d).start())
    for n in (1, 2, 0):
        raw_copy(n).start()
    sources[own_border(dom), :] = halo_send[
        pl.ds(pl.multiple_of(dom * borders, borders), borders), :
    ]
    for n in range(2, 7):
        loads[n].wait()

    expert_of = lax.broadcasted_iota(jnp.int32, (experts, nodes), 0)
    across = lax.broadcasted_iota(jnp.int32, (nodes, nodes), 0)
    along = lax.broadcasted_iota(jnp.int32, (nodes, nodes), 1)
    earlier = jnp.where(across < along, 1.0, 0.0).astype(bf16)

    def tables(chosen, weight, count):
        named = [jnp.where(expert_of == chosen[k : k + 1, :], 1.0, 0.0) for k in range(2)]
        before = dot((named[0] + named[1]).astype(bf16), earlier)
        slot_row = lax.broadcasted_iota(jnp.int32, (count, nodes), 0).astype(f32)
        found = []
        for k in range(2):
            within = jnp.sum(named[k] * before, axis=0, keepdims=True)
            place = chosen[k : k + 1, :]
            place = ((place >> 1) ^ dom) * 2 + (place & 1)
            found.append(jnp.where(slot_row == place.astype(f32) * capacity + within, 1.0, 0.0))
        gate = jnp.sum(
            found[0] * weight[0:1, :] + found[1] * weight[1:2, :], axis=1, keepdims=True
        )
        return found, (found[0] + found[1]).astype(bf16), gate

    slotted, gather, slot_gate = tables(routes[...], route_weight[...], padded)
    gather, slot_gate = gather[0:slots, :], slot_gate[0:slots, :]
    gates = [
        jnp.sum(jnp.where(across == along, route_weight[k : k + 1, :], 0.0), axis=1, keepdims=True)
        for k in range(2)
    ]

    def fill(a, values):
        for d in range(doms):
            part = values[d * block : (d + 1) * block].astype(bf16)
            send[a, d] = part
            if d == 0:
                token[a, 0, 0] = part

    def fill_peer(values):
        for d in range(half):
            part = values[d * block : (d + 1) * block].astype(bf16)
            if d == 0:
                token[0, 2, 0] = part
            else:
                peer_send[d] = part

    fill(0, dot(gather, out_grad[...]) * slot_gate)
    to_core(0, 0).start()

    near_tile = 1 + lax.div(dom, half)
    far_tile = 3 - near_tile

    def adjacency(t):
        found = jnp.zeros((nodes, nodes), f32)
        for s in range(edges.shape[0]):
            found = found + edges[s].astype(f32) * jnp.where(tile_index[0, s] == t, 1.0, 0.0)
        return found

    def tile(t):
        return sources[pl.ds(pl.multiple_of(t * nodes, nodes), nodes), :]

    matrix = [adjacency(t) for t in (0, near_tile, far_tile)]
    degree = 1.0 + jnp.sum(matrix[0] + matrix[1] + matrix[2], axis=1, keepdims=True)
    root = jnp.sqrt(degree)
    summed = own.astype(f32) + dot(matrix[0].astype(bf16), own)
    raw_copy(1).wait_recv()
    raw_copy(2).wait_recv()
    _, peer_gather, peer_gate = tables(peer_routes[...], peer_weight[...], half * block)
    raw_copy(0).wait_recv()
    fill_peer(dot(peer_gather, raw[...]) * peer_gate)
    relayed(0, 0).start()
    loads[7].wait()
    halo_all(half - 1, 0).wait_recv()
    summed = summed + dot(matrix[1].astype(bf16), tile(near_tile))
    halo_all(half, 1).wait_recv()
    summed = summed + dot(matrix[2].astype(bf16), tile(far_tile))
    aggregated = (summed / root).astype(bf16)
    preact = dot(aggregated, gcn[...])
    hidden[...] = (own.astype(f32) + preact / (1.0 + jnp.exp(-preact))).astype(bf16)
    fill(1, dot(gather, hidden[...]))
    each(1, half, lambda d: slot(1, d).start())
    each(half, half + 2, lambda d: slot(1, d).start())
    to_chip(1, 0).start()
    to_core(1, 0).start()

    def pass_two(a, d):
        pass_on(a, d)
        slot(a, d + 2).start()

    loads[8].wait()
    loads[9].wait()
    pass_on(1, 1)
    each(half, half + 2, lambda d: pass_two(1, d))
    pass_near(1)
    to_core(1, 0, half).wait_recv()
    take(1, 0, 0)
    project(0, 0)
    each(half + 2, doms, lambda d: pass_on(1, d))
    each(half, doms, lambda d: slot(0, d).start())
    each(1, half, lambda d: slot(0, d).start())
    each(1, half, lambda d: peer_slot(d).start())
    to_chip(1, 0, half).wait_recv()
    relayed(1, 0, half).start()
    relayed(1, 0, half).wait_recv()
    take(1, 0, 1)
    project(0, 1)
    each(half, half + 2, lambda d: relay(1, d))
    combine(0, 1)
    core_copy(1, 0).start()
    each(half + 2, doms, lambda d: relay(1, d))
    to_core(1, half, half).wait_recv()
    take(1, 1, 0)
    project(1, 0)
    core_copy(1, 0).wait_recv()
    each(0, half, send_sum)
    relayed(1, half, half).wait_recv()
    take(1, 1, 1)
    project(1, 1)
    combine(1, 1)
    core_copy(1, 1).start()
    combine(0, 0)
    core_copy(0, 0).start()
    core_copy(1, 1).wait_recv()
    each(half, doms, send_sum)
    combine(1, 0)
    core_copy(0, 1).start()
    slot(0, 1).wait_recv()
    to_core(0, 1).start()
    pass_near(0)
    pass_peer()
    each(half, doms, lambda d: pass_on(0, d))
    core_copy(0, 0).wait_recv()
    each(1, half, send_back)
    returned[0] = sum_up(0)
    to_core(0, half, half).wait_recv()
    take(0, 1, 0)
    slopes(1, 0)
    to_core(0, 0, half).wait_recv()
    take(0, 0, 0)
    relayed(0, 0, half).wait_recv()
    take(0, 0, 1)
    core_copy(0, 1).wait_recv()
    each(half, half + 2, send_back)
    slopes(0, None)
    weight_grads(0)
    each(half + 2, doms, send_back)
    weight_grads(1)
    each(half, doms, lambda d: relay(0, d))
    relayed(0, half, half).wait_recv()
    take(0, 1, 1)
    slopes(1, 1)

    halo_all(doms - 1, 0).wait_send()
    for a in range(2):
        slot_all(a, 1, doms).wait_send()
        if a == 0:
            peer_slot(1, half - 1).wait_send()
            to_chip(a, half, half).wait_send()
        else:
            to_chip(a, 0, doms).wait_send()
        to_core(a, 0, doms).wait_send()
        relayed(a, 0, doms).wait_send()
    remote(
        partial.at[pl.ds(0, 2)],
        from_core,
        core_ss.at[0],
        core_rs.at[0, 0],
        dom=dom,
        group=other_core,
    ).wait_send()
    remote(total.at[1], from_x, x_ss.at[0], x_rs.at[0], dom=dom, group=other_chip).wait_send()
    for n in range(3):
        raw_copy(n).wait_send()
    ret_copy(1, doms - 1).wait()
    back = jnp.concatenate([returned[d].astype(f32) for d in range(doms)], axis=0).astype(bf16)
    mixed = jnp.zeros((nodes, width), f32)
    for k in range(2):
        mixed = mixed + gates[k] * dot(slotted[k].T[:, 0:slots].astype(bf16), back)
    node_out[...] = (hidden[...].astype(f32) + mixed).astype(bf16)


def fused(
    features,
    out_grad,
    gcn_weight,
    tile_index,
    tile_edges,
    halo_rows,
    routes,
    route_weight,
    up_weight,
    down_weight,
):
    doms = lax.axis_size("dom")
    nodes, width = features.shape
    experts, _, units = up_weight.shape
    capacity = capacity_of(nodes, routes.shape[1], experts * doms)
    border = doms * halo_rows.shape[-1]
    block = experts * capacity
    last_rows = doms * 24
    window_rows = 3 * last_rows
    bf16 = jnp.bfloat16
    dma = pltpu.SemaphoreType.DMA
    whole = pl.BlockSpec(memory_space=pltpu.VMEM)
    away = pl.BlockSpec(memory_space=pl.ANY)
    outs = pl.pallas_call(
        functools.partial(fused_kernel, doms, capacity),
        out_shape=(
            pltpu.VMEM(features.shape, bf16),
            pltpu.VMEM(up_weight.shape, bf16),
            pltpu.VMEM(down_weight.shape, bf16),
            *[pltpu.VMEM((experts, last_rows, size), bf16) for size in (width, width, units, units)],
        ),
        in_specs=[away] * 10,
        out_specs=(whole,) * 7,
        scratch_shapes=[
            pltpu.VMEM(features.shape, bf16),
            pltpu.VMEM(halo_rows.shape[2:], jnp.int32),
            pltpu.VMEM((2, nodes), jnp.int32),
            pltpu.VMEM((2, nodes), jnp.float32),
            pltpu.VMEM(out_grad.shape, bf16),
            pltpu.VMEM(tile_edges.shape[1:], jnp.int32),
            pltpu.SMEM(tile_index.shape, jnp.int32),
            pltpu.VMEM(gcn_weight.shape, bf16),
            pltpu.VMEM(up_weight.shape, bf16),
            pltpu.VMEM(down_weight.shape, bf16),
            pltpu.VMEM((border, width), bf16),
            pltpu.VMEM((nodes + border, width), bf16),
            pltpu.VMEM((2, doms, block, width), bf16),
            pltpu.VMEM((2, 4, doms, block, width), bf16),
            pltpu.VMEM((2, window_rows, width), bf16),
            pltpu.VMEM((2, window_rows, width), bf16),
            pltpu.VMEM((2, window_rows, units), bf16),
            pltpu.VMEM((2, window_rows, units), bf16),
            pltpu.VMEM((4, doms, block, width), bf16),
            pltpu.VMEM((2, doms, block, width), bf16),
            pltpu.VMEM((doms, block, width), bf16),
            pltpu.VMEM((2, doms, block, width), bf16),
            pltpu.VMEM((doms, block, width), bf16),
            pltpu.VMEM((nodes, width), bf16),
            pltpu.VMEM((nodes, width), bf16),
            pltpu.VMEM((2, nodes), jnp.int32),
            pltpu.VMEM((2, nodes), jnp.float32),
            pltpu.VMEM((doms // 2, block, width), bf16),
            dma((10,)),
            dma((1,)),
            dma((2,)),
            dma((2,)),
            dma((2, 2 + doms // 2)),
            dma((2,)),
            dma((2, 1 + doms // 2)),
            dma((2,)),
            dma((2, 2)),
            dma((2,)),
            dma((2, 2)),
            dma((1,)),
            dma((2, 2)),
            dma((1,)),
            dma((doms,)),
            dma((1,)),
            dma((1,)),
            dma((3,)),
            dma((3,)),
            dma((1,)),
            dma((1,)),
        ],
        compiler_params=pltpu.CompilerParams(
            collective_id=0, has_side_effects=True, vmem_limit_bytes=44 * 1024 * 1024
        ),
    )(
        features,
        out_grad,
        gcn_weight,
        tile_index,
        tile_edges[0],
        halo_rows[0, 0],
        routes.T,
        route_weight.T,
        up_weight,
        down_weight,
    )
    return finish(*outs)


def finish_kernel(
    node, up, down, hidden, cot, active, pre, node_out, up_out, down_out, up_sum, down_sum, sems
):
    experts, width, _ = up.shape
    rows = width // 2
    copies = [pltpu.make_async_copy(node, node_out, sems.at[0])]
    copies[0].start()
    parts = ((active, cot, down, down_sum, down_out), (hidden, pre, up, up_sum, up_out))
    for e in range(experts):
        for f in range(2):
            piece = pl.ds(f * rows, rows)
            for left, right, part, total, out in parts:
                added = dot(left[e, :, piece], right[e], ((0,), (0,)))
                total[e, piece, :] = (part[e, piece, :].astype(jnp.float32) + added).astype(out.dtype)
                copy = pltpu.make_async_copy(
                    total.at[e, piece], out.at[e, piece], sems.at[len(copies)]
                )
                copy.start()
                copies.append(copy)
    for copy in copies:
        copy.wait()


def finish(*arrays):
    whole = pl.BlockSpec(memory_space=pltpu.VMEM)
    away = pl.BlockSpec(memory_space=pl.ANY)
    results = arrays[:3]
    return pl.pallas_call(
        finish_kernel,
        out_shape=tuple(jax.ShapeDtypeStruct(a.shape, a.dtype) for a in results),
        in_specs=[whole] * 7,
        out_specs=(away, away, away),
        scratch_shapes=[
            pltpu.VMEM(arrays[1].shape, arrays[1].dtype),
            pltpu.VMEM(arrays[2].shape, arrays[2].dtype),
            pltpu.SemaphoreType.DMA((1 + 4 * arrays[1].shape[0],)),
        ],
        compiler_params=pltpu.CompilerParams(vmem_limit_bytes=24 * 1024 * 1024),
    )(*(pltpu.with_memory_space_constraint(a, pltpu.VMEM) for a in arrays))


def layer(features, out_grad, gcn_weight, tile_index, tile_edges, halo_rows, routes, *rest):
    doms, groups = lax.axis_size("dom"), lax.axis_size("group")
    experts = rest[1].shape[0]
    capacity = capacity_of(features.shape[0], routes.shape[1], experts * doms)
    plain = (
        groups == 4
        and experts == 2
        and routes.shape[1] == 2
        and capacity == 20
        and tile_index.shape[0] == 1
        and features.shape[0] == 128
        and tile_edges.shape[-1] == 128
        and rest[1].shape[1:] == (1024, 1024)
        and experts * doms <= 128
        and halo_rows.shape[-1] % 16 == 0
        and doms * halo_rows.shape[-1] % 128 == 0
        and doms == 8
    )
    body = fused if plain else local
    return body(features, out_grad, gcn_weight, tile_index, tile_edges, halo_rows, routes, *rest)


def solution(mesh):
    in_specs = (
        P(("dom", "group"), None),
        P(("dom", "group"), None),
        P(),
        P(("dom", "group"), None),
        P(("dom", "group"), None, None, None),
        P("dom", "group", None, None),
        P(("dom", "group"), None),
        P(("dom", "group"), None),
        P("dom", None, "group"),
        P("dom", "group", None),
    )
    out_specs = (P(("dom", "group"), None), P("dom", None, "group"), P("dom", "group", None))
    return jax.shard_map(layer, mesh=mesh, in_specs=in_specs, out_specs=out_specs, check_vma=False)
```

```python
import functools

import jax
import jax.numpy as jnp
from jax import lax
from jax.experimental import pallas as pl
from jax.experimental.pallas import tpu as pltpu
from jax.sharding import PartitionSpec as P


def silu_slope(values):
    logistic = jax.nn.sigmoid(values)
    return logistic * (1.0 + values * (1.0 - logistic))


def capacity_of(node_count, top_count, expert_count):
    return max(2, 5 * node_count * top_count // (4 * expert_count))


def slot_table(route_rows, expert_count, capacity):
    flat_ids = route_rows.reshape(-1)
    order = jnp.arange(flat_ids.shape[0], dtype=jnp.int32)
    alike = (flat_ids[:, None] == flat_ids[None, :]) & (order[None, :] < order[:, None])
    within = jnp.sum(alike.astype(jnp.int32), axis=1)
    target = flat_ids * capacity + within
    filler = (
        jnp.zeros((expert_count * capacity,), jnp.int32)
        .at[target]
        .set(jnp.arange(flat_ids.shape[0], dtype=jnp.int32) + 1)
    )
    return (target, filler)


def local(
    features,
    out_grad,
    gcn_weight,
    tile_index,
    tile_edges,
    halo_rows,
    routes,
    route_weight,
    up_weight,
    down_weight,
):
    dom_count = lax.axis_size("dom")
    group_count = lax.axis_size("group")
    node_count, width = features.shape
    tile_rows = tile_edges.shape[-1]
    local_tiles = tile_index.shape[0]
    border_rows = halo_rows.shape[-1]
    expert_local = up_weight.shape[0]
    expert_count = expert_local * dom_count
    top_count = routes.shape[1]
    capacity = capacity_of(node_count, top_count, expert_count)
    send_lists = halo_rows.reshape(-1)
    outgoing = features[send_lists].reshape(dom_count, border_rows, width)
    incoming = lax.all_to_all(outgoing, "dom", split_axis=0, concat_axis=0, tiled=True)
    sources = jnp.concatenate(
        [features, incoming.reshape(dom_count * border_rows, width)], axis=0
    ).reshape(-1, tile_rows, width)
    source_tiles = sources.shape[0]
    listed = (tile_index[:, :, None] == jnp.arange(source_tiles, dtype=jnp.int32)).astype(jnp.int32)
    adjacency = jnp.sum(
        tile_edges[:, :, :, None, :] * listed[:, :, None, :, None], axis=1
    ).reshape(local_tiles, tile_rows, source_tiles * tile_rows)
    summed = features.reshape(local_tiles, tile_rows, width).astype(jnp.float32) + jnp.einsum(
        "tij,jd->tid",
        adjacency.astype(jnp.bfloat16),
        sources.reshape(source_tiles * tile_rows, width),
        preferred_element_type=jnp.float32,
    )
    degree = 1.0 + jnp.sum(tile_edges, axis=(1, 3)).astype(jnp.float32)
    aggregated = (
        (summed / jnp.sqrt(degree)[:, :, None]).reshape(node_count, width).astype(jnp.bfloat16)
    )
    preact = jnp.dot(aggregated, gcn_weight, preferred_element_type=jnp.float32)
    hidden = (features.astype(jnp.float32) + jax.nn.silu(preact)).astype(jnp.bfloat16)
    targets, fillers = slot_table(routes, expert_count, capacity)
    cotangent = (
        (route_weight[:, :, None] * out_grad[:, None, :].astype(jnp.float32))
        .astype(jnp.bfloat16)
        .reshape(-1, width)
    )
    present = (fillers > 0)[:, None]
    source_pair = jnp.maximum(fillers - 1, 0)
    nothing = jnp.zeros((), jnp.bfloat16)
    slot_shape = (dom_count, expert_local * capacity, width)
    send_hidden = jnp.where(present, hidden[source_pair // top_count], nothing).reshape(slot_shape)
    send_cot = jnp.where(present, cotangent[source_pair], nothing).reshape(slot_shape)
    mine_cot = lax.all_to_all(send_cot, "dom", split_axis=0, concat_axis=0, tiled=True)
    token_cot = lax.all_gather(mine_cot[None], "group", axis=0, tiled=True)
    mine_hidden = lax.all_to_all(send_hidden, "dom", split_axis=0, concat_axis=0, tiled=True)
    token_hidden = lax.all_gather(mine_hidden[None], "group", axis=0, tiled=True)
    sender_count = group_count * dom_count
    token_hidden = token_hidden.reshape(sender_count, expert_local, capacity, width)
    token_cot = token_cot.reshape(sender_count, expert_local, capacity, width)
    up_proj = jnp.einsum(
        "secd,edf->secf", token_hidden, up_weight, preferred_element_type=jnp.float32
    )
    active = jax.nn.silu(up_proj).astype(jnp.bfloat16)
    merged = lax.psum_scatter(
        jnp.einsum(
            "secf,efd->secd", active, down_weight, preferred_element_type=jnp.float32
        ).astype(jnp.bfloat16),
        "group",
        scatter_dimension=0,
        tiled=True,
    )
    expert_out = merged.reshape(dom_count, expert_local * capacity, width)
    returned = lax.all_to_all(expert_out, "dom", split_axis=0, concat_axis=0, tiled=True).reshape(
        expert_count * capacity, width
    )
    gathered = returned[targets].reshape(node_count, top_count, width)
    node_out = (
        hidden.astype(jnp.float32)
        + jnp.sum(route_weight[:, :, None] * gathered.astype(jnp.float32), axis=1)
    ).astype(jnp.bfloat16)
    grad_act = jnp.einsum(
        "secd,efd->secf", token_cot, down_weight, preferred_element_type=jnp.float32
    )
    grad_pre = (grad_act * silu_slope(up_proj)).astype(jnp.bfloat16)
    down_grad = jnp.einsum(
        "secf,secd->efd", active, token_cot, preferred_element_type=jnp.float32
    ).astype(jnp.bfloat16)
    up_grad = jnp.einsum(
        "secd,secf->edf", token_hidden, grad_pre, preferred_element_type=jnp.float32
    ).astype(jnp.bfloat16)
    return (node_out, up_grad, down_grad)


def dot(left, right, over=((1,), (0,))):
    return lax.dot_general(left, right, (over, ((), ())), preferred_element_type=jnp.float32)


def fused_kernel(
    doms,
    capacity,
    features_in,
    out_grad_in,
    gcn_weight,
    tile_index_in,
    edges_in,
    halo_rows_in,
    routes_in,
    route_weight_in,
    up_weight,
    down_weight,
    node_out,
    up_grad,
    down_grad,
    last_hidden,
    last_cot,
    last_active,
    last_pre,
    features,
    halo_rows,
    routes,
    route_weight,
    out_grad,
    edges,
    tile_index,
    gcn,
    up,
    down,
    halo_send,
    sources,
    send,
    token,
    rows_hidden,
    rows_cot,
    active,
    grad_pre,
    partial,
    from_core,
    from_x,
    total,
    returned,
    hidden,
    raw,
    peer_routes,
    peer_weight,
    peer_send,
    weight_sem,
    halo_ss,
    halo_rs,
    slot_ss,
    slot_rs,
    fx_ss,
    fx_rs,
    fc_ss,
    fc_rs,
    fd_ss,
    fd_rs,
    core_ss,
    core_rs,
    x_ss,
    x_rs,
    ret_ss,
    ret_rs,
    raw_ss,
    raw_rs,
    peer_ss,
    peer_rs,
):
    f32, bf16 = jnp.float32, jnp.bfloat16
    dom, group = lax.axis_index("dom"), lax.axis_index("group")
    chip, core = group // 2, group % 2
    other_core = chip * 2 + (1 - core)
    other_chip = (1 - chip) * 2 + core
    nodes, width = features.shape
    borders = halo_rows.shape[1]
    block = 2 * capacity
    window = 24
    second = block - window
    slots = doms * block
    padded = -(-slots // 128) * 128
    experts = 2 * doms
    hidden_units = up.shape[2]
    half = doms // 2
    side = half * window
    batch = 2 * side
    step = 512

    def partner(d):
        place = 0
        for bit in (1, 2, 4):
            mine, theirs = lax.rem(lax.div(dom, bit), 2), lax.rem(lax.div(d, bit), 2)
            place = place + bit * (mine + theirs - 2 * mine * theirs)
        return place

    def own_border(place):
        return pl.ds(pl.multiple_of(nodes + place * borders, borders), borders)

    def remote(src, dst, ss, rs, **where):
        return pltpu.make_async_remote_copy(
            src_ref=src,
            dst_ref=dst,
            send_sem=ss,
            recv_sem=rs,
            device_id=where,
            device_id_type=pl.DeviceIdType.MESH,
        )

    def each(low, high, body, unroll=1):
        def one(place, carry):
            body(place)
            return carry

        lax.fori_loop(low, high, one, 0, unroll=unroll)

    def side_of(d):
        return lax.div(d, half)

    def halo_copy(d):
        there = partner(d)
        return remote(
            halo_send.at[pl.ds(pl.multiple_of(there * borders, borders), borders)],
            sources.at[own_border(dom)],
            halo_ss.at[0],
            halo_rs.at[side_of(d)],
            dom=there,
            group=group,
        )

    def halo_all(count, h):
        rows = pl.ds(0, count * borders)
        return remote(
            halo_send.at[rows],
            sources.at[rows],
            halo_ss.at[0],
            halo_rs.at[h],
            dom=dom,
            group=other_core,
        )

    def slot(a, d):
        return remote(
            send.at[a, d],
            token.at[a, 0, d],
            slot_ss.at[a],
            slot_rs.at[a, lax.max(d - half + 2, lax.min(d - 1, 1))],
            dom=partner(d),
            group=group,
        )

    def slot_all(a, low, high):
        chunks = pl.ds(low, high - low)
        return remote(
            send.at[a, chunks],
            token.at[a, 0, chunks],
            slot_ss.at[a],
            slot_rs.at[a, 1],
            dom=dom,
            group=other_core,
        )

    def forward(a, low, count, src, dst, to, ss, rs):
        chunks = pl.ds(low, count)
        return remote(token.at[a, src, chunks], token.at[a, dst, chunks], ss, rs, dom=dom, group=to)

    def to_chip(a, d, count=1):
        return forward(
            a, d, count, 0, 2, other_chip, fx_ss.at[a], fx_rs.at[a, lax.max(d - half + 1, 0)]
        )

    def to_core(a, d, count=1):
        return forward(
            a, d, count, 0, 1, other_core, fc_ss.at[a], fc_rs.at[a, side_of(d)]
        )

    def relayed(a, d, count=1):
        return forward(
            a, d, count, 2, 3, other_core, fd_ss.at[a], fd_rs.at[a, side_of(d)]
        )

    def pass_on(a, d):
        slot(a, d).wait_recv()
        to_chip(a, d).start()
        to_core(a, d).start()

    def raw_copy(n):
        source = (out_grad_in, routes_in, route_weight_in)[n]
        target = (raw, peer_routes, peer_weight)[n]
        return remote(source, target, raw_ss.at[n], raw_rs.at[n], dom=dom, group=other_chip)

    def peer_slot(d, count=1):
        chunks = pl.ds(d, count)
        return remote(
            peer_send.at[chunks],
            token.at[0, 2, chunks],
            peer_ss.at[0],
            peer_rs.at[0],
            dom=partner(d),
            group=group,
        )

    def pass_near(a):
        slot_all(a, 2, half).wait_recv()
        if a == 1:
            to_chip(a, 2, half - 2).start()
        to_core(a, 2, half - 2).start()

    def pass_peer():
        peer_slot(1, half - 1).wait_recv()
        relayed(0, 1, half - 1).start()

    def relay(a, d):
        to_chip(a, d).wait_recv()
        relayed(a, d).start()

    def core_copy(which, h):
        return remote(
            partial.at[1 + 2 * which, pl.ds(h * half, half)],
            from_core.at[which, pl.ds(h * half, half)],
            core_ss.at[0],
            core_rs.at[which, h],
            dom=dom,
            group=other_core,
        )

    def x_copy(d):
        return remote(
            total.at[1, d], from_x.at[d], x_ss.at[0], x_rs.at[d], dom=dom, group=other_chip
        )

    def ret_copy(d, count=1):
        chunks = pl.ds(d, count)
        return remote(
            total.at[0, chunks],
            returned.at[chunks],
            ret_ss.at[0],
            ret_rs.at[0],
            dom=partner(d),
            group=group,
        )

    row_of = lax.broadcasted_iota(jnp.int32, (window, 1), 0)
    keep = [
        jnp.where(row_of < capacity, 1.0, 0.0).astype(bf16),
        jnp.where(row_of >= window - capacity, 1.0, 0.0).astype(bf16),
    ]
    early = lax.broadcasted_iota(jnp.int32, (window - second, 1), 0) < capacity - second

    def place_of(h, c):
        if h == 1 and c == 1:
            return (last_cot, last_hidden, last_active, last_pre), pl.ds(0, batch)
        count = 2 * batch if c is None else batch
        return (rows_cot, rows_hidden, active, grad_pre), pl.ds((2 * h + (c or 0)) * batch, count)

    def take(a, h, c):
        arrays, rows = place_of(h, c)
        for j in range(2):
            start = rows.start + j * side
            for e in range(2):
                parts = []
                for k in range(half):
                    values = token[a, 2 * c + j, h * half + k, e * second : e * second + window, :]
                    if a == 0:
                        values = values * keep[e]
                    parts.append(values)
                arrays[a][e, start : start + side, :] = jnp.concatenate(parts, axis=0)

    def project(h, c, ready=False):
        (_, hidden_of, active_of, pre_of), rows = place_of(h, c)

        def units(f):
            columns = pl.ds(pl.multiple_of(f * step, step), step)
            projs = [dot(hidden_of[e, rows, :], up[e, :, columns]) for e in range(2)]
            for e, proj in enumerate(projs):
                gate = 0.5 + 0.5 * jnp.tanh(0.5 * proj)
                value = proj * gate
                active_of[e, rows, columns] = value.astype(bf16)
                slope = gate + value * (1.0 - gate)
                if ready:
                    slope = slope * pre_of[e, rows, columns].astype(f32)
                pre_of[e, rows, columns] = slope.astype(bf16)

        each(0, hidden_units // step, units, 2)

    def combine(h, c):
        (_, _, active_of, _), rows = place_of(h, c)
        chips = (0, 1) if c is None else (c,)

        def outs(f):
            columns = pl.ds(pl.multiple_of(f * step, step), step)
            first = dot(active_of[0, rows, :], down[0, :, columns])
            last = dot(active_of[1, rows, :], down[1, :, columns])
            for n in range(len(chips) * 2 * half):
                at = n * window
                cut = at + second
                values = jnp.concatenate(
                    [
                        first[at:cut],
                        jnp.where(early, first[cut : at + window], last[at : at + window - second]),
                        last[at + window - second : at + window],
                    ],
                    axis=0,
                )
                rel = 2 * chips[n // (2 * half)] + n // half % 2
                partial[rel, h * half + n % half, :, columns] = values.astype(bf16)

        each(0, width // step, outs, 2)

    def slopes(h, c, first=False):
        (cot_of, _, _, pre_of), rows = place_of(h, c)

        def units(f):
            columns = pl.ds(pl.multiple_of(f * step, step), step)
            grads = [dot(cot_of[e, rows, :], down[e, columns, :], ((1,), (1,))) for e in range(2)]
            for e, grad in enumerate(grads):
                if not first:
                    grad = grad * pre_of[e, rows, columns].astype(f32)
                pre_of[e, rows, columns] = grad.astype(bf16)

        each(0, hidden_units // step, units, 2)

    def weight_grads(e):
        def blocks(f):
            rows = pl.ds(pl.multiple_of(f * 512, 512), 512)
            down_grad[e, rows, :] = dot(active[e, :, rows], rows_cot[e], ((0,), (0,))).astype(bf16)
            up_grad[e, rows, :] = dot(rows_hidden[e, :, rows], grad_pre[e], ((0,), (0,))).astype(bf16)

        each(0, width // 512, blocks, 2)

    def send_sum(d):
        total[1, d] = (partial[2, d].astype(f32) + from_core[1, d].astype(f32)).astype(bf16)
        x_copy(d).start()

    def sum_up(d):
        x_copy(d).wait_recv()
        return (
            partial[0, d].astype(f32) + from_core[0, d].astype(f32) + from_x[d].astype(f32)
        ).astype(bf16)

    def send_back(d):
        total[0, d] = sum_up(d)
        ret_copy(d).start()

    loads = [
        pltpu.make_async_copy(source, target, weight_sem.at[n])
        for n, (source, target) in enumerate(
            (
                (features_in, features),
                (halo_rows_in, halo_rows),
                (routes_in, routes),
                (route_weight_in, route_weight),
                (out_grad_in, out_grad),
                (edges_in, edges),
                (tile_index_in, tile_index),
                (gcn_weight, gcn),
                (up_weight, up),
                (down_weight, down),
            )
        )
    ]
    barrier = pltpu.get_barrier_semaphore()
    each(
        1,
        doms,
        lambda d: pl.semaphore_signal(
            barrier,
            inc=1,
            device_id={"dom": partner(d), "group": group},
            device_id_type=pl.DeviceIdType.MESH,
        ),
    )
    for peer in (other_core, other_chip):
        pl.semaphore_signal(
            barrier,
            inc=1,
            device_id={"dom": dom, "group": peer},
            device_id_type=pl.DeviceIdType.MESH,
        )
    for load in loads:
        load.start()
    loads[0].wait()
    loads[1].wait()
    own = features[...]
    node_of = lax.broadcasted_iota(jnp.int32, (nodes, borders), 0)
    picks = jnp.concatenate(
        [jnp.where(node_of == halo_rows[b : b + 1, :], 1.0, 0.0).T for b in range(doms)], axis=0
    ).astype(bf16)
    halo_send[...] = dot(picks, own).astype(bf16)
    pl.semaphore_wait(barrier, doms + 1)
    each(half, doms, lambda d: halo_copy(d).start())
    each(1, half, lambda d: halo_copy(d).start())
    for n in (1, 2, 0):
        raw_copy(n).start()
    sources[own_border(dom), :] = halo_send[
        pl.ds(pl.multiple_of(dom * borders, borders), borders), :
    ]
    for n in range(2, 7):
        loads[n].wait()

    expert_of = lax.broadcasted_iota(jnp.int32, (experts, nodes), 0)
    across = lax.broadcasted_iota(jnp.int32, (nodes, nodes), 0)
    along = lax.broadcasted_iota(jnp.int32, (nodes, nodes), 1)
    earlier = jnp.where(across < along, 1.0, 0.0).astype(bf16)

    def tables(chosen, weight, count):
        named = [jnp.where(expert_of == chosen[k : k + 1, :], 1.0, 0.0) for k in range(2)]
        before = dot((named[0] + named[1]).astype(bf16), earlier)
        slot_row = lax.broadcasted_iota(jnp.int32, (count, nodes), 0).astype(f32)
        found = []
        for k in range(2):
            within = jnp.sum(named[k] * before, axis=0, keepdims=True)
            place = chosen[k : k + 1, :]
            place = ((place >> 1) ^ dom) * 2 + (place & 1)
            found.append(jnp.where(slot_row == place.astype(f32) * capacity + within, 1.0, 0.0))
        gate = jnp.sum(
            found[0] * weight[0:1, :] + found[1] * weight[1:2, :], axis=1, keepdims=True
        )
        return found, (found[0] + found[1]).astype(bf16), gate

    slotted, gather, slot_gate = tables(routes[...], route_weight[...], padded)
    gather, slot_gate = gather[0:slots, :], slot_gate[0:slots, :]
    gates = [
        jnp.sum(jnp.where(across == along, route_weight[k : k + 1, :], 0.0), axis=1, keepdims=True)
        for k in range(2)
    ]

    def fill(a, values):
        for d in range(doms):
            part = values[d * block : (d + 1) * block].astype(bf16)
            send[a, d] = part
            if d == 0:
                token[a, 0, 0] = part

    def fill_peer(values):
        for d in range(half):
            part = values[d * block : (d + 1) * block].astype(bf16)
            if d == 0:
                token[0, 2, 0] = part
            else:
                peer_send[d] = part

    fill(0, dot(gather, out_grad[...]) * slot_gate)
    to_core(0, 0).start()

    near_tile = 1 + lax.div(dom, half)
    far_tile = 3 - near_tile

    def adjacency(t):
        found = jnp.zeros((nodes, nodes), f32)
        for s in range(edges.shape[0]):
            found = found + edges[s].astype(f32) * jnp.where(tile_index[0, s] == t, 1.0, 0.0)
        return found

    def tile(t):
        return sources[pl.ds(pl.multiple_of(t * nodes, nodes), nodes), :]

    matrix = [adjacency(t) for t in (0, near_tile, far_tile)]
    degree = 1.0 + jnp.sum(matrix[0] + matrix[1] + matrix[2], axis=1, keepdims=True)
    root = jnp.sqrt(degree)
    summed = own.astype(f32) + dot(matrix[0].astype(bf16), own)
    raw_copy(1).wait_recv()
    raw_copy(2).wait_recv()
    _, peer_gather, peer_gate = tables(peer_routes[...], peer_weight[...], half * block)
    raw_copy(0).wait_recv()
    fill_peer(dot(peer_gather, raw[...]) * peer_gate)
    relayed(0, 0).start()
    loads[7].wait()
    halo_all(half - 1, 0).wait_recv()
    summed = summed + dot(matrix[1].astype(bf16), tile(near_tile))
    halo_all(half, 1).wait_recv()
    summed = summed + dot(matrix[2].astype(bf16), tile(far_tile))
    aggregated = (summed / root).astype(bf16)
    preact = dot(aggregated, gcn[...])
    hidden[...] = (own.astype(f32) + preact / (1.0 + jnp.exp(-preact))).astype(bf16)
    fill(1, dot(gather, hidden[...]))
    each(1, half, lambda d: slot(1, d).start())
    each(half, half + 2, lambda d: slot(1, d).start())
    to_chip(1, 0).start()
    to_core(1, 0).start()

    def pass_two(a, d):
        pass_on(a, d)
        slot(a, d + 2).start()

    loads[8].wait()
    loads[9].wait()
    pass_on(1, 1)
    each(half, half + 2, lambda d: pass_two(1, d))
    pass_near(1)
    to_core(1, 0, half).wait_recv()
    take(1, 0, 0)
    project(0, 0)
    each(half + 2, doms, lambda d: pass_on(1, d))
    each(half, doms, lambda d: slot(0, d).start())
    each(1, half, lambda d: slot(0, d).start())
    each(1, half, lambda d: peer_slot(d).start())
    to_chip(1, 0, half).wait_recv()
    relayed(1, 0, half).start()
    relayed(1, 0, half).wait_recv()
    take(1, 0, 1)
    project(0, 1)
    each(half, half + 2, lambda d: relay(1, d))
    combine(0, 1)
    core_copy(1, 0).start()
    each(half + 2, doms, lambda d: relay(1, d))
    to_core(1, half, half).wait_recv()
    take(1, 1, 0)
    project(1, 0)
    core_copy(1, 0).wait_recv()
    each(0, half, send_sum)
    relayed(1, half, half).wait_recv()
    take(1, 1, 1)
    project(1, 1)
    combine(1, 1)
    core_copy(1, 1).start()
    combine(0, 0)
    core_copy(0, 0).start()
    core_copy(1, 1).wait_recv()
    each(half, doms, send_sum)
    combine(1, 0)
    core_copy(0, 1).start()
    slot(0, 1).wait_recv()
    to_core(0, 1).start()
    pass_near(0)
    pass_peer()
    each(half, doms, lambda d: pass_on(0, d))
    core_copy(0, 0).wait_recv()
    each(1, half, send_back)
    returned[0] = sum_up(0)
    to_core(0, half, half).wait_recv()
    take(0, 1, 0)
    slopes(1, 0)
    to_core(0, 0, half).wait_recv()
    take(0, 0, 0)
    relayed(0, 0, half).wait_recv()
    take(0, 0, 1)
    core_copy(0, 1).wait_recv()
    each(half, half + 2, send_back)
    slopes(0, None)
    weight_grads(0)
    each(half + 2, doms, send_back)
    weight_grads(1)
    each(half, doms, lambda d: relay(0, d))
    relayed(0, half, half).wait_recv()
    take(0, 1, 1)
    slopes(1, 1)

    picked = jnp.concatenate([found.T[:, 0:slots].astype(bf16) for found in slotted], axis=0)

    halo_all(doms - 1, 0).wait_send()
    for a in range(2):
        slot_all(a, 1, doms).wait_send()
        if a == 0:
            peer_slot(1, half - 1).wait_send()
            to_chip(a, half, half).wait_send()
        else:
            to_chip(a, 0, doms).wait_send()
        to_core(a, 0, doms).wait_send()
        relayed(a, 0, doms).wait_send()
    remote(
        partial.at[pl.ds(0, 2)],
        from_core,
        core_ss.at[0],
        core_rs.at[0, 0],
        dom=dom,
        group=other_core,
    ).wait_send()
    remote(total.at[1], from_x, x_ss.at[0], x_rs.at[0], dom=dom, group=other_chip).wait_send()
    for n in range(3):
        raw_copy(n).wait_send()
    ret_copy(1, doms - 1).wait()
    back = jnp.concatenate([returned[d].astype(f32) for d in range(doms)], axis=0).astype(bf16)
    both = dot(picked, back)
    mixed = gates[0] * both[0:nodes] + gates[1] * both[nodes:]
    node_out[...] = (hidden[...].astype(f32) + mixed).astype(bf16)


def fused(
    features,
    out_grad,
    gcn_weight,
    tile_index,
    tile_edges,
    halo_rows,
    routes,
    route_weight,
    up_weight,
    down_weight,
):
    doms = lax.axis_size("dom")
    nodes, width = features.shape
    experts, _, units = up_weight.shape
    capacity = capacity_of(nodes, routes.shape[1], experts * doms)
    border = doms * halo_rows.shape[-1]
    block = experts * capacity
    last_rows = doms * 24
    window_rows = 3 * last_rows
    bf16 = jnp.bfloat16
    dma = pltpu.SemaphoreType.DMA
    whole = pl.BlockSpec(memory_space=pltpu.VMEM)
    away = pl.BlockSpec(memory_space=pl.ANY)
    outs = pl.pallas_call(
        functools.partial(fused_kernel, doms, capacity),
        out_shape=(
            pltpu.VMEM(features.shape, bf16),
            pltpu.VMEM(up_weight.shape, bf16),
            pltpu.VMEM(down_weight.shape, bf16),
            *[pltpu.VMEM((experts, last_rows, size), bf16) for size in (width, width, units, units)],
        ),
        in_specs=[away] * 10,
        out_specs=(whole,) * 7,
        scratch_shapes=[
            pltpu.VMEM(features.shape, bf16),
            pltpu.VMEM(halo_rows.shape[2:], jnp.int32),
            pltpu.VMEM((2, nodes), jnp.int32),
            pltpu.VMEM((2, nodes), jnp.float32),
            pltpu.VMEM(out_grad.shape, bf16),
            pltpu.VMEM(tile_edges.shape[1:], jnp.int32),
            pltpu.SMEM(tile_index.shape, jnp.int32),
            pltpu.VMEM(gcn_weight.shape, bf16),
            pltpu.VMEM(up_weight.shape, bf16),
            pltpu.VMEM(down_weight.shape, bf16),
            pltpu.VMEM((border, width), bf16),
            pltpu.VMEM((nodes + border, width), bf16),
            pltpu.VMEM((2, doms, block, width), bf16),
            pltpu.VMEM((2, 4, doms, block, width), bf16),
            pltpu.VMEM((2, window_rows, width), bf16),
            pltpu.VMEM((2, window_rows, width), bf16),
            pltpu.VMEM((2, window_rows, units), bf16),
            pltpu.VMEM((2, window_rows, units), bf16),
            pltpu.VMEM((4, doms, block, width), bf16),
            pltpu.VMEM((2, doms, block, width), bf16),
            pltpu.VMEM((doms, block, width), bf16),
            pltpu.VMEM((2, doms, block, width), bf16),
            pltpu.VMEM((doms, block, width), bf16),
            pltpu.VMEM((nodes, width), bf16),
            pltpu.VMEM((nodes, width), bf16),
            pltpu.VMEM((2, nodes), jnp.int32),
            pltpu.VMEM((2, nodes), jnp.float32),
            pltpu.VMEM((doms // 2, block, width), bf16),
            dma((10,)),
            dma((1,)),
            dma((2,)),
            dma((2,)),
            dma((2, 2 + doms // 2)),
            dma((2,)),
            dma((2, 1 + doms // 2)),
            dma((2,)),
            dma((2, 2)),
            dma((2,)),
            dma((2, 2)),
            dma((1,)),
            dma((2, 2)),
            dma((1,)),
            dma((doms,)),
            dma((1,)),
            dma((1,)),
            dma((3,)),
            dma((3,)),
            dma((1,)),
            dma((1,)),
        ],
        compiler_params=pltpu.CompilerParams(
            collective_id=0, has_side_effects=True, vmem_limit_bytes=44 * 1024 * 1024
        ),
    )(
        features,
        out_grad,
        gcn_weight,
        tile_index,
        tile_edges[0],
        halo_rows[0, 0],
        routes.T,
        route_weight.T,
        up_weight,
        down_weight,
    )
    return finish(*outs)


def finish_kernel(
    node, up, down, hidden, cot, active, pre, node_out, up_out, down_out, up_sum, down_sum, sems
):
    experts, width, _ = up.shape
    rows = width // 4
    copies = [pltpu.make_async_copy(node, node_out, sems.at[0])]
    copies[0].start()
    parts = ((active, cot, down, down_sum, down_out), (hidden, pre, up, up_sum, up_out))
    for e in range(experts):
        for f in range(4):
            piece = pl.ds(f * rows, rows)
            for left, right, part, total, out in parts:
                added = dot(left[e, :, piece], right[e], ((0,), (0,)))
                total[e, piece, :] = (part[e, piece, :].astype(jnp.float32) + added).astype(out.dtype)
                copy = pltpu.make_async_copy(
                    total.at[e, piece], out.at[e, piece], sems.at[len(copies)]
                )
                copy.start()
                copies.append(copy)
    for copy in copies:
        copy.wait()


def finish(*arrays):
    whole = pl.BlockSpec(memory_space=pltpu.VMEM)
    away = pl.BlockSpec(memory_space=pl.ANY)
    results = arrays[:3]
    return pl.pallas_call(
        finish_kernel,
        out_shape=tuple(jax.ShapeDtypeStruct(a.shape, a.dtype) for a in results),
        in_specs=[whole] * 7,
        out_specs=(away, away, away),
        scratch_shapes=[
            pltpu.VMEM(arrays[1].shape, arrays[1].dtype),
            pltpu.VMEM(arrays[2].shape, arrays[2].dtype),
            pltpu.SemaphoreType.DMA((1 + 8 * arrays[1].shape[0],)),
        ],
        compiler_params=pltpu.CompilerParams(vmem_limit_bytes=24 * 1024 * 1024),
    )(*(pltpu.with_memory_space_constraint(a, pltpu.VMEM) for a in arrays))


def layer(features, out_grad, gcn_weight, tile_index, tile_edges, halo_rows, routes, *rest):
    doms, groups = lax.axis_size("dom"), lax.axis_size("group")
    experts = rest[1].shape[0]
    capacity = capacity_of(features.shape[0], routes.shape[1], experts * doms)
    plain = (
        groups == 4
        and experts == 2
        and routes.shape[1] == 2
        and capacity == 20
        and tile_index.shape[0] == 1
        and features.shape[0] == 128
        and tile_edges.shape[-1] == 128
        and rest[1].shape[1:] == (1024, 1024)
        and experts * doms <= 128
        and halo_rows.shape[-1] % 16 == 0
        and doms * halo_rows.shape[-1] % 128 == 0
        and doms == 8
    )
    body = fused if plain else local
    return body(features, out_grad, gcn_weight, tile_index, tile_edges, halo_rows, routes, *rest)


def solution(mesh):
    in_specs = (
        P(("dom", "group"), None),
        P(("dom", "group"), None),
        P(),
        P(("dom", "group"), None),
        P(("dom", "group"), None, None, None),
        P("dom", "group", None, None),
        P(("dom", "group"), None),
        P(("dom", "group"), None),
        P("dom", None, "group"),
        P("dom", "group", None),
    )
    out_specs = (P(("dom", "group"), None), P("dom", None, "group"), P("dom", "group", None))
    return jax.shard_map(layer, mesh=mesh, in_specs=in_specs, out_specs=out_specs, check_vma=False)
```
